32 devices in a mesh: ka: 16 (over z, x, core), ga: 2 (over y).
Axes of the slice: x: 2, y: 2, z: 4, core: 2. Of those that a mesh axis runs over, the one named last changes fastest.
Arguments:
- pair_density: bfloat16 [256, 64, 4096], P('ka', None, 'ga'), may hold values from -0.1875 to 0.1875
- trial_vectors: bfloat16 [256, 64, 128], P('ka'), may hold values from -6 to 6
- energy: float32 [256, 64], P('ka'), may hold values from 0.5 to 2.5
- coulomb: float32 [4096], P('ga'), may hold values from 0.03 to 0.3
- screen: bfloat16 [32, 4096, 256], P(None, 'ga'), may hold values from -0.375 to 0.375
- neighbors: int32 [256, 16], P('ka'), may hold values from 0 to 255, as said below
- live_count: int32 [256], P('ka'), may hold values from 1 to 16, as said below
- q_index: int32 [256, 16], P('ka'), may hold values from 0 to 31
Outputs:
- applied: bfloat16 [256, 64, 128], P('ka', 'ga')
The draws below stay inside these ranges and needn't reach their ends.
Inputs may be any that keep to these rules, and one draw needn't show every extreme that they name: `neighbors`: the 16 partners of k-point k are distinct k-points whose block k' // 16 is the block of k or one of its two neighbours on the closed cycle of 16 blocks. Only the first live_count[k] slots of row k of neighbors and q_index are used; some k-point uses all 16.
All inputs are finite; a program needn't handle non-finite values.
Results may differ from the reference program's by a relative error of at most 0.013.
Values may be sent and summed in bfloat16 or wider, within the bound.
No kernel may reach another device: no remote copies, remote signals or barrier semaphores. Data moves between devices by JAX's collectives and lax.ppermute only.
A program may use at most 192 MiB of HBM per device.

```python
import math
import jax
import jax.numpy as jnp
from jax import lax

P_SIZE = 64
NG = 4096
NT = 128
BW = 256
NQ = 32
NB = 16
K_DEV = 16
NK = 256


def draw_neighbors(key, part):
    cycle_size = NK // K_DEV
    row_keys = jax.random.split(key, NK)

    def one_row(k_index, row_key):
        shuffled = jax.random.permutation(row_key, 3 * K_DEV)[:NB]
        home_block = (k_index // K_DEV + shuffled // K_DEV - 1) % cycle_size
        return (home_block * K_DEV + shuffled % K_DEV).astype(jnp.int32)
    return jax.vmap(one_row)(jnp.arange(NK, dtype=jnp.int32), row_keys)


def draw_live_count(key, part):
    cap_key, count_key = jax.random.split(key)
    cycle_size = NK // K_DEV
    block_caps = jax.random.randint(cap_key, (cycle_size,), max(NB // 4, 1), NB + 1)
    block_caps = jnp.where(jnp.arange(cycle_size) == 0, NB, block_caps)
    raw_draw = jax.random.randint(count_key, (NK,), 0, 1 << 20)
    counts = 1 + raw_draw % jnp.repeat(block_caps, K_DEV)
    return jnp.where(jnp.arange(NK) == 0, NB, counts).astype(jnp.int32)


def place_ends(drawn, own_key, least, largest):
    dims = drawn.shape
    place = [jax.random.randint(jax.random.fold_in(own_key, axis), (), 0, dims[axis]) for axis in range(len(dims))]
    drawn = drawn.at[tuple(place)].set(least)
    longest = dims.index(max(dims))
    place[longest] = (place[longest] + 1) % dims[longest]
    return drawn.at[tuple(place)].set(largest)


def with_spikes(drawn, stream_key, source, target, shards_of, factor):
    owner, partner = [(jnp.arange(drawn.shape[axis_at]) // (drawn.shape[axis_at] // shards_of)).reshape([-1 if axis == axis_at else 1 for axis in range(drawn.ndim)]) for axis_at in (source, target)]
    chosen = jax.random.permutation(stream_key, shards_of)[partner]
    strong = (owner == chosen) | (owner == (partner + shards_of // 2) % shards_of)
    return jnp.where(strong, factor * drawn, drawn)


def levels(own_key, dims, cuts, low, largest):
    loudness, own = 1.0, jax.random.fold_in(own_key, 6)
    for axis_at, shards_of in cuts:
        heights = jnp.exp(jax.random.uniform(jax.random.fold_in(own, axis_at), (shards_of,), jnp.float32, low / len(cuts), largest / len(cuts)))
        loudness = loudness * jnp.repeat(heights, dims[axis_at] // shards_of).reshape([-1 if axis == axis_at else 1 for axis in range(len(dims))])
    return loudness


def normal_values(key, shape, width, most, cuts=(), kind=jnp.bfloat16):
    factor_of = levels(key, shape, cuts, -0.22, 0.18) if cuts else 1.0
    array = jax.random.normal(key, shape, jnp.float32) * width * factor_of
    return jnp.minimum(jnp.maximum(array, -most), most).astype(kind)


def heavy_noise(key, shape, deviation, limit, cuts, heavy, kind=jnp.bfloat16):
    result = deviation * jax.random.normal(key, shape, jnp.float32)
    if cuts:
        result = result * levels(key, shape, cuts, -0.22, 0.18)
    return jnp.clip(with_spikes(result, jax.random.fold_in(key, 3), *heavy), -limit, limit).astype(kind)


def setup_inputs(seed: int = 0) -> dict:
    streams_of = jax.random.split(jax.random.key(seed), 9)
    pair_density = heavy_noise(streams_of[0], (NK, P_SIZE, NG), (2.0 * NG ** -0.5), 0.1875, ((0, 16), (2, 2)), (2, 1, 2, 2.0))
    trial_vectors = normal_values(streams_of[1], (NK, P_SIZE, NT), 1.0, 6.0, ((0, 16),))
    energy = jnp.clip(0.5 + 2.0 * jax.random.uniform(streams_of[2], (NK, P_SIZE), jnp.float32) ** levels(streams_of[2], (NK, P_SIZE), ((0, 16),), -0.2, 0.2), 0.5, 2.5)
    coulomb = jnp.clip(jnp.exp(math.log(0.3) - 2.3025852 * jax.random.uniform(streams_of[3], (NG,), jnp.float32) ** levels(streams_of[3], (NG,), ((0, 2),), -0.2, 0.2)), 0.03, 0.3)
    screen = normal_values(streams_of[4], (NQ, NG, BW), BW ** -0.5, 0.375, ((1, 2),))
    neighbors = draw_neighbors(jax.random.fold_in(streams_of[8], 71), 0)
    live_count = draw_live_count(jax.random.fold_in(streams_of[8], 71), 0)
    q_index = place_ends(jax.random.randint(streams_of[7], (NK, NB), 0, NQ), jax.random.fold_in(streams_of[7], 1), 0, NQ - 1).astype(jnp.int32)
    return {"pair_density": pair_density, "trial_vectors": trial_vectors, "energy": energy, "coulomb": coulomb, "screen": screen, "neighbors": neighbors, "live_count": live_count, "q_index": q_index}


def reference(pair_density, trial_vectors, energy, coulomb, screen, neighbors, live_count, q_index):
    def make_product(items):
        density, vectors = items
        return jnp.dot(density.T, vectors, preferred_element_type=jnp.float32).astype(jnp.bfloat16)

    products = lax.map(make_product, (pair_density, trial_vectors))

    def add_k(carry, item):
        return carry + item.astype(jnp.float32), None

    density_total, _ = lax.scan(add_k, jnp.zeros((NG, NT), jnp.float32), products)
    screened = coulomb[:, None] * density_total
    groups = NG // BW

    def apply_k(items):
        density, nbr_row, q_row, count = items

        def add_slot(slot_index, summed):
            picked = products[nbr_row[slot_index]].astype(jnp.float32).reshape(groups, BW, NT)
            block = screen[q_row[slot_index]].astype(jnp.float32).reshape(groups, BW, BW)
            coupled = jnp.einsum('bgc,bct->bgt', block, picked).reshape(NG, NT)
            return summed + jnp.where(slot_index < count, coupled, 0.0)

        direct = lax.fori_loop(0, NB, add_slot, jnp.zeros((NG, NT), jnp.float32))
        kernel = (2.0 * screened - direct).astype(jnp.bfloat16)
        return jnp.dot(density, kernel, preferred_element_type=jnp.float32)

    pair_terms = lax.map(apply_k, (pair_density, neighbors, q_index, live_count))
    return (energy[:, :, None] * trial_vectors.astype(jnp.float32) + pair_terms).astype(jnp.bfloat16)
```

```python
import jax
import jax.numpy as jnp
from jax import lax
from jax.experimental import pallas as pl
from jax.experimental.pallas import tpu as pltpu
from jax.sharding import PartitionSpec as P

UNROLL = 16
F32, BF16 = jnp.float32, jnp.bfloat16


def pair_list(n_slot, k_slot, q, valid, q_count, length, spare):
    entries = q.shape[0]
    order = jnp.arange(entries, dtype=jnp.int32)
    qs = jnp.arange(q_count, dtype=jnp.int32)
    same = (q[:, None] == q[None, :]) & valid[None, :] & (order[None, :] < order[:, None])
    within = jnp.sum(same.astype(jnp.int32), axis=1)
    count = jnp.sum(((q[None, :] == qs[:, None]) & valid[None, :]).astype(jnp.int32), axis=1)
    padded = (count + 1) // 2 * 2
    base = jnp.sum(jnp.where(qs[None, :] < q[:, None], padded[None, :], 0), axis=1)
    place = jnp.where(valid, base + within, -1)
    code = n_slot + 64 * k_slot + 4096 * q
    blank = 64 * spare
    rows = jnp.arange(length, dtype=jnp.int32)
    listed = blank + jnp.sum(jnp.where(place[None, :] == rows[:, None], code[None, :] - blank, 0), axis=1)
    rounds = (jnp.sum(padded) + UNROLL - 1) // UNROLL
    return listed, rounds[None]


def couple_kernel(listed, rounds, group, x_ref, y_ref, tx_ref, ty_ref, w_ref, acc_ref, out_ref, prod, total):
    half = x_ref.shape[0]
    width = x_ref.shape[2]
    trials = tx_ref.shape[1]

    @pl.when(pl.program_id(0) == 0)
    def _():
        out_ref[...] = acc_ref[...]

    for ref, vec, first in ((x_ref, tx_ref, 0), (y_ref, ty_ref, half)):

        def make(i, _, ref=ref, vec=vec, first=first):
            for d in range(8):
                n = i * 8 + d
                made = jnp.dot(vec[n], ref[n], preferred_element_type=F32)
                prod[first + n] = made.astype(BF16)
            return 0

        lax.fori_loop(0, half // 8, make, 0)
    total[...] = jnp.zeros_like(total)

    def some(i, _):
        for d in range(0, UNROLL, 2):
            a, b = listed[i * UNROLL + d], listed[i * UNROLL + d + 1]
            both = jnp.concatenate([prod[a & 63], prod[b & 63]], axis=0)
            made = lax.dot_general(both, w_ref[a >> 12], (((1,), (1,)), ((), ())), preferred_element_type=F32)
            total[(a >> 6) & 63] += made[:trials]
            total[(b >> 6) & 63] += made[trials:]
        return 0

    lax.fori_loop(0, rounds[0], some, 0)
    for ref, first in ((x_ref, 0), (y_ref, half)):

        def close(i, _, ref=ref, first=first):
            for d in range(8):
                k = i * 8 + d
                out_ref[first + k] += lax.dot_general(
                    ref[k], total[first + k].astype(BF16), (((1,), (1,)), ((), ())), preferred_element_type=F32
                )
            return 0

        lax.fori_loop(0, half // 8, close, 0)


def couple(listed, rounds, first_group, x, y, tx, ty, screen, acc, groups):
    half, pairs, _ = x.shape
    trials = tx.shape[1]
    q_count, _, width = screen.shape
    slots = 2 * half
    chunk = pl.BlockSpec((half, pairs, width), lambda i, *_: (0, 0, i))
    whole_t = pl.BlockSpec((half, trials, pairs), lambda i, *_: (0, 0, 0))
    sums = pl.BlockSpec((slots, pairs, trials), lambda i, *_: (0, 0, 0))
    work = groups * 2 * 128 * width * width * trials
    return pl.pallas_call(
        couple_kernel,
        out_shape=jax.ShapeDtypeStruct((slots, pairs, trials), F32),
        grid_spec=pltpu.PrefetchScalarGridSpec(
            num_scalar_prefetch=3,
            grid=(groups,),
            in_specs=[
                chunk,
                chunk,
                whole_t,
                whole_t,
                pl.BlockSpec((q_count, width, width), lambda i, l, r, g: (0, g[0] + i, 0)),
                sums,
            ],
            out_specs=sums,
            scratch_shapes=[
                pltpu.VMEM((slots, trials, width), BF16),
                pltpu.VMEM((slots + 1, trials, width), F32),
            ],
        ),
        compiler_params=pltpu.CompilerParams(vmem_limit_bytes=48 << 20),
        cost_estimate=pl.CostEstimate(
            flops=2 * work, transcendentals=0, bytes_accessed=groups * q_count * width * width * 2
        ),
    )(listed, rounds, first_group, x, y, tx, ty, screen, acc)


def ring_sum(part, me, size):
    steps = []
    bit = 2
    while bit < size:
        steps.append(bit)
        bit *= 2
    for bit in steps:
        rows = part.shape[0] // 2
        high = (me // bit) % 2
        keep = lax.dynamic_slice_in_dim(part, high * rows, rows, 0)
        give = lax.dynamic_slice_in_dim(part, (1 - high) * rows, rows, 0).astype(BF16)
        part = keep + lax.ppermute(give, "ka", [(i, i ^ bit) for i in range(size)]).astype(F32)
    part = part.astype(BF16)
    for bit in reversed(steps):
        high = (me // bit) % 2
        other = lax.ppermute(part, "ka", [(i, i ^ bit) for i in range(size)])
        part = jnp.where(high == 0, jnp.concatenate([part, other], 0), jnp.concatenate([other, part], 0))
    return part


def on_device(pair_density, trial_vectors, energy, coulomb, screen, neighbors, live_count, q_index):
    local_k, pair_count, local_g = pair_density.shape
    trial_count = trial_vectors.shape[2]
    q_count, _, width = screen.shape
    slots = neighbors.shape[1]
    size, parts = lax.axis_size("ka"), lax.axis_size("ga")
    me, mine = lax.axis_index("ka"), lax.axis_index("ga")
    core = me % 2
    half_g = local_g // 2
    groups = half_g // width
    first_block = me - core
    sibling = [(i, i ^ 1) for i in range(size)]
    onward = [(i, (i + 2) % size) for i in range(size)]

    def by_block(own, other):
        return jnp.where(core == 0, own, other), jnp.where(core == 0, other, own)

    own_half = lax.dynamic_slice_in_dim(pair_density, core * half_g, half_g, 2)
    give_half = lax.dynamic_slice_in_dim(pair_density, (1 - core) * half_g, half_g, 2)
    dens_a, dens_b = by_block(own_half, lax.ppermute(give_half, "ka", sibling))
    table = jnp.concatenate([neighbors, q_index, live_count[:, None]], axis=1)
    table_a, table_b = by_block(table, lax.ppermute(table, "ka", sibling))
    vec_a, vec_b = by_block(trial_vectors, lax.ppermute(trial_vectors, "ka", sibling))

    quarter = local_k // 2
    vec_half = lax.ppermute(lax.dynamic_slice_in_dim(vec_b, core * quarter, quarter, 0), "ka", onward)
    table_p = lax.ppermute(table_b, "ka", onward)
    chunks = [
        lax.ppermute(dens_b[:, :, c * width : (c + 1) * width], "ka", onward) for c in range(groups)
    ]
    vec_other = lax.ppermute(vec_half, "ka", sibling)
    vec_p = jnp.where(
        core == 0, jnp.concatenate([vec_half, vec_other], 0), jnp.concatenate([vec_other, vec_half], 0)
    )

    part = sum(
        lax.dot_general(d, v, (((0, 1), (0, 1)), ((), ())), preferred_element_type=F32)
        for d, v in ((dens_a, vec_a), (dens_b, vec_b))
    )
    density_total = ring_sum(part, me, size)
    my_coulomb = lax.dynamic_slice_in_dim(coulomb, core * half_g, half_g, 0)
    screened2 = (2.0 * my_coulomb[:, None] * density_total.astype(F32)).astype(BF16)

    def columns(t):
        live = jnp.arange(slots, dtype=jnp.int32)[None, :] < t[:, 2 * slots :]
        near = t[:, :slots]
        return near // local_k, near % local_k, t[:, slots : 2 * slots], live

    row = jnp.broadcast_to(jnp.arange(local_k, dtype=jnp.int32)[:, None], (local_k, slots))
    blk_a, in_a, q_a, live_a = columns(table_a)
    blk_b, in_b, q_b, live_b = columns(table_b)
    blk_p, in_p, q_p, live_p = columns(table_p)
    flat = lambda u, v: jnp.concatenate([u.reshape(-1), v.reshape(-1)])
    last_block = first_block + 1
    before = (first_block + size - 1) % size
    length = 2 * local_k * slots + q_count
    length = (length + UNROLL - 1) // UNROLL * UNROLL
    here = lambda blk, live: live & ((blk == first_block) | (blk == last_block))
    near_list, near_rounds = pair_list(
        flat(in_a + local_k * (blk_a == last_block), in_b + local_k * (blk_b == last_block)),
        flat(row, row + local_k),
        flat(q_a, q_b),
        flat(here(blk_a, live_a), here(blk_b, live_b)),
        q_count,
        length,
        2 * local_k,
    )
    far_list, far_rounds = pair_list(
        flat(in_a + local_k, in_p),
        flat(row, row + local_k),
        flat(q_a, q_p),
        flat(live_a & (blk_a == before), live_p & (blk_p == first_block)),
        q_count,
        length,
        2 * local_k,
    )

    turned = lambda v: jnp.swapaxes(v, 1, 2)
    tv_a, tv_b, tv_p = turned(vec_a), turned(vec_b), turned(vec_p)
    start = (core * groups).astype(jnp.int32)
    zero = jnp.zeros((2 * local_k, pair_count, trial_count), F32)
    near = couple(near_list, near_rounds, start[None], dens_a, dens_b, tv_a, tv_b, screen, zero, groups)
    far = zero
    for c in range(groups):
        part_a = dens_a[:, :, c * width : (c + 1) * width]
        far = couple(
            far_list, far_rounds, (start + c)[None], part_a, chunks[c], tv_a, tv_p, screen, far, 1
        )
    exchange_a, exchange_b = (
        lax.dot_general(d, screened2, (((2,), (0,)), ((), ())), preferred_element_type=F32)
        for d in (dens_a, dens_b)
    )
    sum_a = exchange_a - near[:local_k] - far[:local_k]
    sum_b = exchange_b - near[local_k:]
    sum_p = -far[local_k:]

    got = lax.ppermute(jnp.where(core == 0, sum_b, sum_a).astype(BF16), "ka", sibling).astype(F32)
    own = jnp.where(core == 0, sum_a, sum_b) + got
    passed = lax.ppermute(sum_p.astype(BF16), "ka", [(i, i + 1) for i in range(0, size, 2)])
    back = sum_p + passed.astype(F32)
    rows = pair_count // parts

    def sent(value, steps, ka_pairs):
        rows_of = lax.dynamic_slice_in_dim(value, ((mine + steps) % parts) * rows, rows, 1)
        pairs = [
            (s * parts + g, d * parts + (g + steps) % parts) for s, d in ka_pairs for g in range(parts)
        ]
        return lax.ppermute(rows_of.astype(BF16), ("ka", "ga"), pairs).astype(F32)

    stay = [(i, i) for i in range(size)]
    back_pairs = [(i, (i - 2) % size) for i in range(1, size, 2)]
    answer = lax.dynamic_slice_in_dim(own, mine * rows, rows, 1)
    for steps in range(1, parts):
        answer = answer + sent(own, steps, stay)
    for steps in range(parts):
        answer = answer + sent(back, steps, back_pairs)
    energy_rows = lax.dynamic_slice_in_dim(energy, mine * rows, rows, 1)
    vector_rows = lax.dynamic_slice_in_dim(trial_vectors, mine * rows, rows, 1)
    return (energy_rows[:, :, None] * vector_rows.astype(F32) + answer).astype(BF16)


def solution(mesh):
    in_specs = (
        P("ka", None, "ga"),
        P("ka", None, None),
        P("ka", None),
        P("ga"),
        P(None, "ga", None),
        P("ka", None),
        P("ka"),
        P("ka", None),
    )
    out_specs = P("ka", "ga", None)
    return jax.shard_map(
        on_device, mesh=mesh, in_specs=in_specs, out_specs=out_specs, check_vma=False
    )
```

```python
import functools

import jax
import jax.numpy as jnp
from jax import lax
from jax.experimental import pallas as pl
from jax.experimental.pallas import tpu as pltpu
from jax.sharding import PartitionSpec as P

UNROLL = 32
F32, BF16 = jnp.float32, jnp.bfloat16
VMEM, SMEM = pltpu.VMEM, pltpu.SMEM
IN_VMEM, IN_SMEM, ANYWHERE = (pl.BlockSpec(memory_space=space) for space in (VMEM, SMEM, pl.ANY))


def pair_list(n_slot, k_slot, q, valid, q_count, length, spare):
    entries = q.shape[0]
    order = jnp.arange(entries, dtype=jnp.int32)
    qs = jnp.arange(q_count, dtype=jnp.int32)
    same = (q[:, None] == q[None, :]) & valid[None, :] & (order[None, :] < order[:, None])
    within = jnp.sum(same.astype(jnp.int32), axis=1)
    count = jnp.sum(((q[None, :] == qs[:, None]) & valid[None, :]).astype(jnp.int32), axis=1)
    padded = (count + 1) // 2 * 2
    base = jnp.sum(jnp.where(qs[None, :] < q[:, None], padded[None, :], 0), axis=1)
    place = jnp.where(valid, base + within, -1)
    code = n_slot + 64 * k_slot + 4096 * q
    blank = 64 * spare
    rows = jnp.arange(length, dtype=jnp.int32)
    listed = blank + jnp.sum(jnp.where(place[None, :] == rows[:, None], code[None, :] - blank, 0), axis=1)
    rounds = (jnp.sum(padded) + UNROLL - 1) // UNROLL
    return listed, rounds[None]


def dot_last(u, v):
    return lax.dot_general(u, v, (((1,), (1,)), ((), ())), preferred_element_type=F32)


def one_group(listed, rounds, w_ref, row, slabs, vectors, out_ref, prod, total, first):
    trials = prod.shape[1]
    width = prod.shape[2]
    slots = prod.shape[0]

    for n in range(slots):
        made = lax.dot_general(vectors(n), slabs(n), (((0,), (0,)), ((), ())), preferred_element_type=F32)
        prod[n] = made.astype(BF16)
    total[...] = jnp.zeros_like(total)

    def some(i, _):
        for d in range(0, UNROLL, 2):
            a, b = listed[i * UNROLL + d], listed[i * UNROLL + d + 1]
            both = jnp.concatenate([prod[a & 63], prod[b & 63]], axis=0)
            made = dot_last(both, w_ref[a >> 12, pl.ds(row, width), :])
            total[(a >> 6) & 63] += made[:trials]
            total[(b >> 6) & 63] += made[trials:]
        return 0

    lax.fori_loop(0, rounds[0], some, 0)
    for k in range(slots):
        made = dot_last(slabs(k), total[k].astype(BF16))

        if first:
            out_ref[k] = made
        else:
            out_ref[k] += made


def near_kernel(start, count, load, *refs):
    if load:
        core, listed, rounds, own, vec, sib, screen, out, w, prod, total, sems = refs
    else:
        core, listed, rounds, own, vec, sib, w, _, out, prod, total = refs
    half, _, _ = own.shape
    width = prod.shape[2]
    half_g = w.shape[1]
    groups = half_g // width
    own_at = core[0] * half_g

    def copy(g):
        return pltpu.make_async_copy(
            screen.at[:, pl.ds(pl.multiple_of(own_at + g * width, width), width), :],
            w.at[:, pl.ds(g * width, width), :],
            sems.at[g],
        )

    if load:
        for g in range(groups):
            copy(g).start()
    for g in range(start, start + count):
        if load:
            copy(g).wait()
        at = pl.multiple_of(own_at + g * width, width)

        def slabs(n, at=at, g=g):
            return own[n, :, pl.ds(at, width)] if n < half else sib[n - half, :, g * width : (g + 1) * width]

        def vectors(n):
            return vec[n] if n < half else sib[n - half, :, half_g:]

        one_group(listed, rounds, w, g * width, slabs, vectors, out, prod, total, load and g == start)
    if load:
        for g in range(start + count, groups):
            copy(g).wait()


def far_kernel(start, count, fresh, core, listed, rounds, own, vec, sib, w, came0, came1, vec_p, *refs):
    if fresh:
        out, prod, total, came, sem = refs
    else:
        _, out, prod, total, came, sem = refs
    half, _, _ = own.shape
    width = prod.shape[2]
    half_g = w.shape[1]
    own_at = core[0] * half_g

    @pl.when(core[0] == 0)
    def _():
        pltpu.make_async_copy(came0.at[:, :, : count * width], came, sem).start()

    @pl.when(core[0] != 0)
    def _():
        pltpu.make_async_copy(came1.at[:, :, : count * width], came, sem).start()

    pltpu.make_async_copy(came0.at[:, :, : count * width], came, sem).wait()
    for g in range(start, start + count):
        at = pl.multiple_of(own_at + g * width, width)

        def slabs(n, at=at, g=g):
            if n >= half:
                return came[n - half, :, (g - start) * width : (g - start + 1) * width]
            return jnp.where(
                core[0] == 0, own[n, :, pl.ds(at, width)], sib[n, :, g * width : (g + 1) * width]
            )

        def vectors(n):
            if n >= half:
                return vec_p[n - half]
            return jnp.where(core[0] == 0, vec[n], sib[n, :, half_g:])

        one_group(listed, rounds, w, g * width, slabs, vectors, out, prod, total, fresh and g == start)


def last_kernel(core, own, sib, s2, near, far, give, keep):
    half, pairs, _ = own.shape
    trials, half_g = s2.shape
    width = 256
    own_at = core[0] * half_g

    def exchange(slab):
        acc = jnp.zeros((half * pairs, trials), F32)
        for g in range(half_g // width):
            acc += dot_last(slab(g).reshape(half * pairs, width), s2[:, g * width : (g + 1) * width])
        return acc.reshape(half, pairs, trials)

    mine = exchange(lambda g: own[:, :, pl.ds(pl.multiple_of(own_at + g * width, width), width)]) - near[:half]
    other = exchange(lambda g: sib[:, :, g * width : (g + 1) * width]) - near[half:]

    @pl.when(core[0] == 0)
    def _():
        keep[:half] = mine - far[:half]
        keep[half:] = other
        give[:half] = (-far[half:]).astype(BF16)
        give[half:] = other.astype(BF16)

    @pl.when(core[0] != 0)
    def _():
        keep[:half] = -far[half:]
        keep[half:] = mine
        give[:half] = (other - far[:half]).astype(BF16)
        give[half:] = mine.astype(BF16)


def density_sum(part, me, size):
    columns = part.shape[1] // 2
    swap = lambda v, bit: lax.ppermute(v, "ka", [(i, i ^ bit) for i in range(size)])
    high = (me // 2) % 2
    keep = lax.dynamic_slice_in_dim(part, high * columns, columns, 1)
    give = lax.dynamic_slice_in_dim(part, (1 - high) * columns, columns, 1).astype(BF16)
    part = keep + swap(give, 2).astype(F32)
    bit = 4
    while bit < size:
        part = part + swap(part.astype(BF16), bit).astype(F32)
        bit *= 2
    part = part.astype(BF16)
    other = swap(part, 2)
    return jnp.where(high == 0, jnp.concatenate([part, other], 1), jnp.concatenate([other, part], 1))


def on_device(pair_density, trial_vectors, energy, coulomb, screen, neighbors, live_count, q_index):
    local_k, pair_count, local_g = pair_density.shape
    trial_count = trial_vectors.shape[2]
    q_count, _, width = screen.shape
    slots = neighbors.shape[1]
    size, parts = lax.axis_size("ka"), lax.axis_size("ga")
    me, mine = lax.axis_index("ka"), lax.axis_index("ga")
    core = me % 2
    core_id = core.astype(jnp.int32)[None]
    half_g = local_g // 2
    groups = half_g // width
    first_block = me - core
    sibling = [(i, i ^ 1) for i in range(size)]
    onward = [(i, (i + 2) % size) for i in range(size)]
    chunk_count = 2 if groups % 2 == 0 else 1
    chunk_groups = groups // chunk_count
    chunk = chunk_groups * width

    table = jnp.concatenate([neighbors, q_index, live_count[:, None]], axis=1)
    table_s = lax.ppermute(table, "ka", sibling)
    give_half = lax.dynamic_slice_in_dim(pair_density, (1 - core) * half_g, half_g, 2)
    sib = lax.ppermute(jnp.concatenate([give_half, trial_vectors], 2), "ka", sibling)
    came = []
    for c in range(chunk_count):
        pieces = []
        for target in range(2):
            piece = lax.slice_in_dim(
                pair_density, target * half_g + c * chunk, target * half_g + (c + 1) * chunk, axis=2
            )
            if c == 0:
                piece = jnp.concatenate([piece, trial_vectors], 2)
            pieces.append(
                lax.ppermute(piece, "ka", [(i, (i + 1 + target) % size) for i in range(1, size, 2)])
            )
        came.append(pieces)
    table_a = jnp.where(core == 0, table, table_s)
    table_b = jnp.where(core == 0, table_s, table)
    table_p = lax.ppermute(table_b, "ka", onward)

    own_half = lax.dynamic_slice_in_dim(pair_density, core * half_g, half_g, 2)
    contract = lambda v, d: lax.dot_general(v, d, (((0, 1), (0, 1)), ((), ())), preferred_element_type=F32)
    part = contract(trial_vectors, own_half) + contract(sib[:, :, half_g:], sib[:, :, :half_g])
    density_total = density_sum(part, me, size)
    my_coulomb = lax.dynamic_slice_in_dim(coulomb, core * half_g, half_g, 0)
    screened2 = (2.0 * my_coulomb[None, :] * density_total.astype(F32)).astype(BF16)

    def columns(t):
        live = jnp.arange(slots, dtype=jnp.int32)[None, :] < t[:, 2 * slots :]
        near = t[:, :slots]
        return near // local_k, near % local_k, t[:, slots : 2 * slots], live

    row = jnp.broadcast_to(jnp.arange(local_k, dtype=jnp.int32)[:, None], (local_k, slots))
    flat = lambda u, v: jnp.concatenate([u.reshape(-1), v.reshape(-1)])
    other_block = me + 1 - 2 * core
    before = (first_block + size - 1) % size
    length = 2 * local_k * slots + q_count
    length = (length + UNROLL - 1) // UNROLL * UNROLL

    def listing(u, v, u_slot, v_slot, u_valid, v_valid):
        return pair_list(
            flat(u_slot, v_slot),
            flat(row, row + local_k),
            flat(u[2], v[2]),
            flat(u[3] & u_valid, v[3] & v_valid),
            q_count,
            length,
            2 * local_k,
        )

    own_t, sib_t, a_t, p_t = columns(table), columns(table_s), columns(table_a), columns(table_p)
    here = lambda blk: (blk == me) | (blk == other_block)
    near_list, near_rounds = listing(
        own_t,
        sib_t,
        own_t[1] + local_k * (own_t[0] == other_block),
        sib_t[1] + local_k * (sib_t[0] == other_block),
        here(own_t[0]),
        here(sib_t[0]),
    )
    far_list, far_rounds = listing(
        a_t, p_t, a_t[1] + local_k, p_t[1], a_t[0] == before, p_t[0] == first_block
    )

    sums = jax.ShapeDtypeStruct((2 * local_k, pair_count, trial_count), F32)
    work = [
        VMEM((2 * local_k, trial_count, width), BF16),
        VMEM((2 * local_k + 1, trial_count, width), F32),
    ]

    def params():
        return pltpu.CompilerParams(vmem_limit_bytes=20 << 20)

    def cost(count, pairs):
        return pl.CostEstimate(
            flops=4 * count * pairs * width * width * trial_count, transcendentals=0, bytes_accessed=1 << 20
        )

    near_groups = (groups + 1) // 2
    near, w_half = pl.pallas_call(
        functools.partial(near_kernel, 0, near_groups, True),
        out_shape=(sums, jax.ShapeDtypeStruct((q_count, half_g, width), BF16)),
        in_specs=[IN_SMEM, IN_SMEM, IN_SMEM, IN_VMEM, IN_VMEM, IN_VMEM, ANYWHERE],
        out_specs=(IN_VMEM, IN_VMEM),
        scratch_shapes=work + [pltpu.SemaphoreType.DMA((groups,))],
        compiler_params=params(),
        cost_estimate=cost(near_groups, 160),
    )(core_id, near_list, near_rounds, pair_density, trial_vectors, sib, screen)
    if groups > near_groups:
        near = pl.pallas_call(
            functools.partial(near_kernel, near_groups, groups - near_groups, False),
            out_shape=sums,
            in_specs=[IN_SMEM, IN_SMEM, IN_SMEM, IN_VMEM, IN_VMEM, IN_VMEM, IN_VMEM, IN_VMEM],
            out_specs=IN_VMEM,
            scratch_shapes=work,
            input_output_aliases={7: 0},
            compiler_params=params(),
            cost_estimate=cost(groups - near_groups, 160),
        )(core_id, near_list, near_rounds, pair_density, trial_vectors, sib, w_half, near)
    vec_p = jnp.where(core == 0, came[0][0][:, :, chunk:], came[0][1][:, :, chunk:])
    far = None
    for c in range(chunk_count):
        far = pl.pallas_call(
            functools.partial(far_kernel, c * chunk_groups, chunk_groups, c == 0),
            out_shape=sums,
            in_specs=[IN_SMEM, IN_SMEM, IN_SMEM, IN_VMEM, IN_VMEM, IN_VMEM, IN_VMEM, ANYWHERE, ANYWHERE, IN_VMEM]
            + [IN_VMEM] * (c > 0),
            out_specs=IN_VMEM,
            scratch_shapes=work + [VMEM((local_k, pair_count, chunk), BF16), pltpu.SemaphoreType.DMA],
            input_output_aliases={10: 0} if c else {},
            compiler_params=params(),
            cost_estimate=cost(chunk_groups, 80),
        )(
            core_id, far_list, far_rounds, pair_density, trial_vectors, sib, w_half, came[c][0], came[c][1], vec_p,
            *([far] if c else []),
        )
    give, keep = pl.pallas_call(
        last_kernel,
        out_shape=(jax.ShapeDtypeStruct(sums.shape, BF16), sums),
        in_specs=[IN_SMEM] + [IN_VMEM] * 5,
        out_specs=(IN_VMEM, IN_VMEM),
        compiler_params=params(),
        cost_estimate=cost(1, 16),
    )(core_id, pair_density, sib, screened2, near, far)

    both = keep + lax.ppermute(give, "ka", sibling).astype(F32)
    edge, inner = both[:local_k], both[local_k:]
    rows = pair_count // parts
    rows_of = lambda value, at: lax.dynamic_slice_in_dim(value, at * rows, rows, 1)
    stay = lambda first: [(i, i) for i in range(first, size, 2)]
    back = [(i, (i - 2) % size) for i in range(1, size, 2)]

    def sent(value, steps, ka_pairs):
        pairs = [
            (s * parts + g, d * parts + (g + steps) % parts) for s, d in ka_pairs for g in range(parts)
        ]
        return lax.ppermute(
            rows_of(value, (mine + steps) % parts).astype(BF16), ("ka", "ga"), pairs
        ).astype(F32)

    answer = jnp.where(core == 0, rows_of(edge, mine), rows_of(inner, mine))
    answer = answer + sent(edge, 0, back)
    for steps in range(1, parts):
        answer = answer + sent(edge, steps, stay(0) + back) + sent(inner, steps, stay(1))
    energy_rows = lax.dynamic_slice_in_dim(energy, mine * rows, rows, 1)
    vector_rows = lax.dynamic_slice_in_dim(trial_vectors, mine * rows, rows, 1)
    return (energy_rows[:, :, None] * vector_rows.astype(F32) + answer).astype(BF16)


def solution(mesh):
    in_specs = (
        P("ka", None, "ga"),
        P("ka", None, None),
        P("ka", None),
        P("ga"),
        P(None, "ga", None),
        P("ka", None),
        P("ka"),
        P("ka", None),
    )
    out_specs = P("ka", "ga", None)
    return jax.shard_map(
        on_device, mesh=mesh, in_specs=in_specs, out_specs=out_specs, check_vma=False
    )
```

```python
import functools

import jax
import jax.numpy as jnp
from jax import lax
from jax.experimental import pallas as pl
from jax.experimental.pallas import tpu as pltpu
from jax.sharding import PartitionSpec as P

UNROLL = 32
F32, BF16 = jnp.float32, jnp.bfloat16
VMEM, SMEM = pltpu.VMEM, pltpu.SMEM
IN_VMEM, IN_SMEM, ANYWHERE = (pl.BlockSpec(memory_space=space) for space in (VMEM, SMEM, pl.ANY))


def pair_list(n_slot, k_slot, q, valid, q_count, length, spare):
    entries = q.shape[0]
    order = jnp.arange(entries, dtype=jnp.int32)
    qs = jnp.arange(q_count, dtype=jnp.int32)
    same = (q[:, None] == q[None, :]) & valid[None, :] & (order[None, :] < order[:, None])
    within = jnp.sum(same.astype(jnp.int32), axis=1)
    count = jnp.sum(((q[None, :] == qs[:, None]) & valid[None, :]).astype(jnp.int32), axis=1)
    padded = (count + 1) // 2 * 2
    base = jnp.sum(jnp.where(qs[None, :] < q[:, None], padded[None, :], 0), axis=1)
    place = jnp.where(valid, base + within, -1)
    code = n_slot + 64 * k_slot + 4096 * q
    blank = 64 * spare
    rows = jnp.arange(length, dtype=jnp.int32)
    listed = blank + jnp.sum(jnp.where(place[None, :] == rows[:, None], code[None, :] - blank, 0), axis=1)
    rounds = (jnp.sum(padded) + UNROLL - 1) // UNROLL
    return listed, rounds[None]


def dot_last(u, v):
    return lax.dot_general(u, v, (((1,), (1,)), ((), ())), preferred_element_type=F32)


def one_group(listed, rounds, w_ref, row, slabs, vectors, out_ref, prod, total, first):
    trials = prod.shape[1]
    width = prod.shape[2]
    slots = prod.shape[0]

    for n in range(slots):
        made = lax.dot_general(vectors(n), slabs(n), (((0,), (0,)), ((), ())), preferred_element_type=F32)
        prod[n] = made.astype(BF16)
    total[...] = jnp.zeros_like(total)

    def some(i, _):
        for d in range(0, UNROLL, 2):
            a, b = listed[i * UNROLL + d], listed[i * UNROLL + d + 1]
            both = jnp.concatenate([prod[a & 63], prod[b & 63]], axis=0)
            made = dot_last(both, w_ref[a >> 12, pl.ds(row, width), :])
            total[(a >> 6) & 63] += made[:trials]
            total[(b >> 6) & 63] += made[trials:]
        return 0

    lax.fori_loop(0, rounds[0], some, 0)
    for k in range(slots):
        made = dot_last(slabs(k), total[k].astype(BF16))

        if first:
            out_ref[k] = made
        else:
            out_ref[k] += made


def near_kernel(start, count, load, *refs):
    if load:
        core, listed, rounds, own, vec, sib, vec_s, screen, out, w, prod, total, sems = refs
    else:
        core, listed, rounds, own, vec, sib, vec_s, w, _, out, prod, total = refs
    half, _, _ = own.shape
    width = prod.shape[2]
    half_g = w.shape[1]
    groups = half_g // width
    own_at = core[0] * half_g

    def copy(g):
        return pltpu.make_async_copy(
            screen.at[:, pl.ds(pl.multiple_of(own_at + g * width, width), width), :],
            w.at[:, pl.ds(g * width, width), :],
            sems.at[g],
        )

    if load:
        for g in range(groups):
            copy(g).start()
    for g in range(start, start + count):
        if load:
            copy(g).wait()
        at = pl.multiple_of(own_at + g * width, width)

        def slabs(n, at=at, g=g):
            return own[n, :, pl.ds(at, width)] if n < half else sib[n - half, :, g * width : (g + 1) * width]

        def vectors(n):
            return vec[n] if n < half else vec_s[n - half]

        one_group(listed, rounds, w, g * width, slabs, vectors, out, prod, total, load and g == start)
    if load:
        for g in range(start + count, groups):
            copy(g).wait()


def far_kernel(start, count, fresh, sources, core, listed, rounds, own, vec, sib, vec_s, w, vec_p, *refs):
    refs = refs[0 if fresh else 1 :]
    sources, (out, prod, total, came, sem) = refs[:sources], refs[sources:]
    half, _, _ = own.shape
    width = prod.shape[2]
    half_g = w.shape[1]
    own_at = core[0] * half_g
    if len(sources) == 1:
        pltpu.make_async_copy(sources[0], came, sem).start()
    else:

        @pl.when(core[0] == 0)
        def _():
            pltpu.make_async_copy(sources[0], came, sem).start()

        @pl.when(core[0] != 0)
        def _():
            pltpu.make_async_copy(sources[1], came, sem).start()

    pltpu.make_async_copy(sources[0], came, sem).wait()
    for g in range(start, start + count):
        at = pl.multiple_of(own_at + g * width, width)

        def slabs(n, at=at, g=g):
            if n >= half:
                return came[n - half, :, (g - start) * width : (g - start + 1) * width]
            return jnp.where(
                core[0] == 0, own[n, :, pl.ds(at, width)], sib[n, :, g * width : (g + 1) * width]
            )

        def vectors(n):
            if n >= half:
                return vec_p[n - half]
            return jnp.where(core[0] == 0, vec[n], vec_s[n])

        one_group(listed, rounds, w, g * width, slabs, vectors, out, prod, total, fresh and g == start)


def last_kernel(core, own, sib, s2, near, far, give, keep):
    half, pairs, _ = own.shape
    half_g, trials = s2.shape
    width = 256
    own_at = core[0] * half_g

    def exchange(slab):
        acc = jnp.zeros((half * pairs, trials), F32)
        for g in range(half_g // width):
            flat = slab(g).reshape(half * pairs, width)
            acc += jnp.dot(flat, s2[g * width : (g + 1) * width], preferred_element_type=F32)
        return acc.reshape(half, pairs, trials)

    mine = exchange(lambda g: own[:, :, pl.ds(pl.multiple_of(own_at + g * width, width), width)]) - near[:half]
    other = exchange(lambda g: sib[:, :, g * width : (g + 1) * width]) - near[half:]

    @pl.when(core[0] == 0)
    def _():
        keep[:half] = mine - far[:half]
        keep[half:] = other
        give[:half] = (-far[half:]).astype(BF16)
        give[half:] = other.astype(BF16)

    @pl.when(core[0] != 0)
    def _():
        keep[:half] = -far[half:]
        keep[half:] = mine
        give[:half] = (other - far[:half]).astype(BF16)
        give[half:] = mine.astype(BF16)


def density_steps(part, me, size):
    rows = part.shape[0] // 2
    high = (me // 2) % 2
    keep = lax.dynamic_slice_in_dim(part, high * rows, rows, 0)
    part = keep + (yield lax.dynamic_slice_in_dim(part, (1 - high) * rows, rows, 0).astype(BF16), 2).astype(F32)
    bit = 4
    while bit < size:
        part = part + (yield part.astype(BF16), bit).astype(F32)
        bit *= 2
    part = part.astype(BF16)
    other = yield part, 2
    return jnp.where(high == 0, jnp.concatenate([part, other], 0), jnp.concatenate([other, part], 0))


class Density:
    def __init__(self, steps, size):
        self.steps, self.size, self.result = steps, size, None
        self.send(None)

    def send(self, got):
        try:
            self.give, self.bit = self.steps.send(got)
        except StopIteration as stop:
            self.give, self.result = stop.value, stop.value

    def after(self, value):
        if self.result is None:
            came = lax.ppermute(self.give, "ka", [(i, i ^ self.bit) for i in range(self.size)])
            came, value = lax.optimization_barrier((came, value))
            self.send(came)
        return self.before(value)

    def before(self, value):
        self.give, value = lax.optimization_barrier((self.give, value))
        return value

    def finish(self):
        while self.result is None:
            self.after(jnp.zeros((1,), F32))
        return self.give


def on_device(pair_density, trial_vectors, energy, coulomb, screen, neighbors, live_count, q_index):
    local_k, pair_count, local_g = pair_density.shape
    trial_count = trial_vectors.shape[2]
    q_count, _, width = screen.shape
    slots = neighbors.shape[1]
    size, parts = lax.axis_size("ka"), lax.axis_size("ga")
    me, mine = lax.axis_index("ka"), lax.axis_index("ga")
    core = me % 2
    core_id = core.astype(jnp.int32)[None]
    half_g = local_g // 2
    groups = half_g // width
    sibling = [(i, i ^ 1) for i in range(size)]
    onward = [(i, (i + 2) % size) for i in range(size)]
    to_next = [[(i, (i + 1 + target) % size) for i in range(1, size, 2)] for target in range(2)]

    def pick(first, second):
        return jnp.where(core == 0, first, second)

    offset = (neighbors // local_k - me + 1) % size
    table = jnp.concatenate([offset * local_k + neighbors % local_k, q_index, live_count[:, None]], axis=1)
    table_s = lax.ppermute(table, "ka", sibling)
    vec_s = lax.ppermute(trial_vectors, "ka", sibling)
    table_p, vec_p = (
        pick(*(lax.ppermute(value, "ka", pairs) for pairs in to_next)) for value in (table, trial_vectors)
    )

    give_half = lax.dynamic_slice_in_dim(pair_density, (1 - core) * half_g, half_g, 2)
    sib = lax.ppermute(give_half, "ka", sibling)
    own_half = lax.dynamic_slice_in_dim(pair_density, core * half_g, half_g, 2)
    lead = max(groups // 2, 1)
    chunks = [(0, lead)] + [(g, 1) for g in range(lead, groups)]
    came = [
        [
            lax.ppermute(pair_density[:, :, low : low + lead * width], "ka", pairs)
            for low, pairs in zip((0, half_g), to_next)
        ]
    ]
    sending = [
        pick(sib[:, :, g * width : (g + 1) * width], own_half[:, :, g * width : (g + 1) * width])
        for g in range(lead, groups)
    ]
    came += [[lax.ppermute(piece, "ka", onward)] for piece in sending]

    contract = lambda v, d: lax.dot_general(d, v, (((0, 1), (0, 1)), ((), ())), preferred_element_type=F32)
    part = contract(trial_vectors, own_half) + contract(vec_s, sib)
    density = Density(density_steps(part, me, size), size)
    my_coulomb = lax.dynamic_slice_in_dim(coulomb, core * half_g, half_g, 0)

    def columns(t):
        live = jnp.arange(slots, dtype=jnp.int32)[None, :] < t[:, 2 * slots :]
        near = t[:, :slots]
        return near // local_k, near % local_k, t[:, slots : 2 * slots], live

    row = jnp.broadcast_to(jnp.arange(local_k, dtype=jnp.int32)[:, None], (local_k, slots))
    flat = lambda u, v: jnp.concatenate([u.reshape(-1), v.reshape(-1)])
    length = 2 * local_k * slots + q_count
    length = (length + UNROLL - 1) // UNROLL * UNROLL

    def listing(u, v, u_slot, v_slot, u_valid, v_valid):
        return pair_list(
            flat(u_slot, v_slot),
            flat(row, row + local_k),
            flat(u[2], v[2]),
            flat(u[3] & u_valid, v[3] & v_valid),
            q_count,
            length,
            2 * local_k,
        )

    own_t, sib_t = columns(table), columns(table_s)
    own_cross, sib_cross = own_t[0] == 2 - 2 * core, sib_t[0] == 2 * core
    near_list, near_rounds = listing(
        own_t,
        sib_t,
        own_t[1] + local_k * own_cross,
        sib_t[1] + local_k * (sib_t[0] == 1),
        own_cross | (own_t[0] == 1),
        sib_cross | (sib_t[0] == 1),
    )
    a_t, p_t = columns(pick(table, table_s)), columns(table_p)
    far_list, far_rounds = listing(a_t, p_t, a_t[1] + local_k, p_t[1], a_t[0] == 0, p_t[0] == 2)

    sums = jax.ShapeDtypeStruct((2 * local_k, pair_count, trial_count), F32)
    work = [
        VMEM((2 * local_k, trial_count, width), BF16),
        VMEM((2 * local_k + 1, trial_count, width), F32),
    ]

    def params():
        return pltpu.CompilerParams(vmem_limit_bytes=20 << 20)

    def cost(count, pairs):
        return pl.CostEstimate(
            flops=4 * count * pairs * width * width * trial_count, transcendentals=0, bytes_accessed=1 << 20
        )

    near_groups = (groups + 1) // 2
    near_rounds, vec_p, far_list, far_rounds, *_ = lax.optimization_barrier(
        (near_rounds, vec_p, far_list, far_rounds, *sending)
    )
    near_rounds = density.before(near_rounds)
    near, w_half = pl.pallas_call(
        functools.partial(near_kernel, 0, near_groups, True),
        out_shape=(sums, jax.ShapeDtypeStruct((q_count, half_g, width), BF16)),
        in_specs=[IN_SMEM] * 3 + [IN_VMEM] * 4 + [ANYWHERE],
        out_specs=(IN_VMEM, IN_VMEM),
        scratch_shapes=work + [pltpu.SemaphoreType.DMA((groups,))],
        compiler_params=params(),
        cost_estimate=cost(near_groups, 160),
    )(core_id, near_list, near_rounds, pair_density, trial_vectors, sib, vec_s, screen)
    near = density.after(near)
    if groups > near_groups:
        near = pl.pallas_call(
            functools.partial(near_kernel, near_groups, groups - near_groups, False),
            out_shape=sums,
            in_specs=[IN_SMEM] * 3 + [IN_VMEM] * 6,
            out_specs=IN_VMEM,
            scratch_shapes=work,
            input_output_aliases={8: 0},
            compiler_params=params(),
            cost_estimate=cost(groups - near_groups, 160),
        )(core_id, near_list, near_rounds, pair_density, trial_vectors, sib, vec_s, w_half, near)
        near = density.after(near)
    near, far_rounds = lax.optimization_barrier((near, far_rounds))
    far_rounds = density.before(far_rounds)
    far = None
    for c, (start, count) in enumerate(chunks):
        far = pl.pallas_call(
            functools.partial(far_kernel, start, count, c == 0, len(came[c])),
            out_shape=sums,
            in_specs=[IN_SMEM] * 3 + [IN_VMEM] * (6 + (c > 0)) + [ANYWHERE] * len(came[c]),
            out_specs=IN_VMEM,
            scratch_shapes=work
            + [VMEM((local_k, pair_count, count * width), BF16), pltpu.SemaphoreType.DMA],
            input_output_aliases={9: 0} if c else {},
            compiler_params=params(),
            cost_estimate=cost(count, 80),
        )(
            core_id, far_list, far_rounds, pair_density, trial_vectors, sib, vec_s, w_half, vec_p,
            *([far] if c else []), *came[c],
        )
        if c + 1 < len(chunks):
            far = density.after(far)
    screened2 = (2.0 * my_coulomb[:, None] * density.finish().astype(F32)).astype(BF16)
    give, keep = pl.pallas_call(
        last_kernel,
        out_shape=(jax.ShapeDtypeStruct(sums.shape, BF16), sums),
        in_specs=[IN_SMEM] + [IN_VMEM] * 5,
        out_specs=(IN_VMEM, IN_VMEM),
        compiler_params=params(),
        cost_estimate=cost(1, 16),
    )(core_id, pair_density, sib, screened2, near, far)

    both = keep + lax.ppermute(give, "ka", sibling).astype(F32)
    edge, inner = both[:local_k], both[local_k:]
    rows = pair_count // parts
    rows_of = lambda value, at: lax.dynamic_slice_in_dim(value, at * rows, rows, 1)
    stay = lambda first: [(i, i) for i in range(first, size, 2)]
    back = [(i, (i - 2) % size) for i in range(1, size, 2)]

    def sent(value, steps, ka_pairs):
        pairs = [
            (s * parts + g, d * parts + (g + steps) % parts) for s, d in ka_pairs for g in range(parts)
        ]
        return lax.ppermute(
            rows_of(value, (mine + steps) % parts).astype(BF16), ("ka", "ga"), pairs
        ).astype(F32)

    answer = jnp.where(core == 0, rows_of(edge, mine), rows_of(inner, mine))
    answer = answer + sent(edge, 0, back)
    for steps in range(1, parts):
        answer = answer + sent(edge, steps, stay(0) + back) + sent(inner, steps, stay(1))
    energy_rows = lax.dynamic_slice_in_dim(energy, mine * rows, rows, 1)
    vector_rows = lax.dynamic_slice_in_dim(trial_vectors, mine * rows, rows, 1)
    return (energy_rows[:, :, None] * vector_rows.astype(F32) + answer).astype(BF16)


def solution(mesh):
    in_specs = (
        P("ka", None, "ga"),
        P("ka", None, None),
        P("ka", None),
        P("ga"),
        P(None, "ga", None),
        P("ka", None),
        P("ka"),
        P("ka", None),
    )
    out_specs = P("ka", "ga", None)
    return jax.shard_map(
        on_device, mesh=mesh, in_specs=in_specs, out_specs=out_specs, check_vma=False
    )
```

```python
import functools

import jax
import jax.numpy as jnp
from jax import lax
from jax.experimental import pallas as pl
from jax.experimental.pallas import tpu as pltpu
from jax.sharding import PartitionSpec as P

UNROLL = 32
F32, BF16 = jnp.float32, jnp.bfloat16
VMEM, SMEM = pltpu.VMEM, pltpu.SMEM
IN_VMEM, IN_SMEM, ANYWHERE = (pl.BlockSpec(memory_space=space) for space in (VMEM, SMEM, pl.ANY))


def pair_list(n_slot, k_slot, q, valid, q_count, length, spare):
    entries = q.shape[0]
    order = jnp.arange(entries, dtype=jnp.int32)
    qs = jnp.arange(q_count, dtype=jnp.int32)
    same = (q[:, None] == q[None, :]) & valid[None, :] & (order[None, :] < order[:, None])
    within = jnp.sum(same.astype(jnp.int32), axis=1)
    count = jnp.sum(((q[None, :] == qs[:, None]) & valid[None, :]).astype(jnp.int32), axis=1)
    padded = (count + 1) // 2 * 2
    base = jnp.sum(jnp.where(qs[None, :] < q[:, None], padded[None, :], 0), axis=1)
    place = jnp.where(valid, base + within, -1)
    code = n_slot + 64 * k_slot + 4096 * q
    blank = 64 * spare
    rows = jnp.arange(length, dtype=jnp.int32)
    listed = blank + jnp.sum(jnp.where(place[None, :] == rows[:, None], code[None, :] - blank, 0), axis=1)
    rounds = (jnp.sum(padded) + UNROLL - 1) // UNROLL
    return listed, rounds[None]


def dot_last(u, v):
    return lax.dot_general(u, v, (((1,), (1,)), ((), ())), preferred_element_type=F32)


def one_group(listed, rounds, w_ref, row, slabs, vectors, out_ref, prod, total, first):
    trials = prod.shape[1]
    width = prod.shape[2]
    slots = prod.shape[0]

    for n in range(slots):
        made = lax.dot_general(vectors(n), slabs(n), (((0,), (0,)), ((), ())), preferred_element_type=F32)
        prod[n] = made.astype(BF16)
    total[...] = jnp.zeros_like(total)

    def some(i, _):
        for d in range(0, UNROLL, 2):
            a, b = listed[i * UNROLL + d], listed[i * UNROLL + d + 1]
            both = jnp.concatenate([prod[a & 63], prod[b & 63]], axis=0)
            made = dot_last(both, w_ref[a >> 12, pl.ds(row, width), :])
            total[(a >> 6) & 63] += made[:trials]
            total[(b >> 6) & 63] += made[trials:]
        return 0

    lax.fori_loop(0, rounds[0], some, 0)
    for k in range(slots):
        made = dot_last(slabs(k), total[k].astype(BF16))

        if first:
            out_ref[k] = made
        else:
            out_ref[k] += made


def pack_kernel(core, source, *refs):
    outs, sems = refs[:-1], refs[-1]
    half_g, size = source.shape[2] // 2, outs[0].shape[2]
    if len(outs) == 1:
        starts = [pl.multiple_of((1 - core[0]) * half_g, size)]
    else:
        starts = [0, half_g]
    copies = [
        pltpu.make_async_copy(source.at[:, :, pl.ds(start, size)], out, sems.at[i])
        for i, (start, out) in enumerate(zip(starts, outs))
    ]
    for copy in copies:
        copy.start()
    for copy in copies:
        copy.wait()


def near_kernel(start, count, load, *refs):
    if load:
        core, listed, rounds, own, vec, sib, vec_s, screen, out, w, prod, total, sems = refs
    else:
        core, listed, rounds, own, vec, sib, vec_s, w, _, out, prod, total = refs
    half, _, _ = own.shape
    width = prod.shape[2]
    half_g = w.shape[1]
    groups = half_g // width
    own_at = core[0] * half_g

    def copy(g):
        return pltpu.make_async_copy(
            screen.at[:, pl.ds(pl.multiple_of(own_at + g * width, width), width), :],
            w.at[:, pl.ds(g * width, width), :],
            sems.at[g],
        )

    if load:
        for g in range(groups):
            copy(g).start()
    for g in range(start, start + count):
        if load:
            copy(g).wait()
        at = pl.multiple_of(own_at + g * width, width)

        def slabs(n, at=at, g=g):
            return own[n, :, pl.ds(at, width)] if n < half else sib[n - half, :, g * width : (g + 1) * width]

        def vectors(n):
            return vec[n] if n < half else vec_s[n - half]

        one_group(listed, rounds, w, g * width, slabs, vectors, out, prod, total, load and g == start)
    if load:
        for g in range(start + count, groups):
            copy(g).wait()


def far_kernel(start, count, fresh, sources, core, listed, rounds, own, vec, sib, vec_s, w, vec_p, *refs):
    refs = refs[0 if fresh else 1 :]
    sources, (out, prod, total, came, sem) = refs[:sources], refs[sources:]
    half, _, _ = own.shape
    width = prod.shape[2]
    half_g = w.shape[1]
    own_at = core[0] * half_g
    if len(sources) == 1:
        pltpu.make_async_copy(sources[0], came, sem).start()
    else:

        @pl.when(core[0] == 0)
        def _():
            pltpu.make_async_copy(sources[0], came, sem).start()

        @pl.when(core[0] != 0)
        def _():
            pltpu.make_async_copy(sources[1], came, sem).start()

    pltpu.make_async_copy(sources[0], came, sem).wait()
    for g in range(start, start + count):
        at = pl.multiple_of(own_at + g * width, width)

        def slabs(n, at=at, g=g):
            if n >= half:
                return came[n - half, :, (g - start) * width : (g - start + 1) * width]
            return jnp.where(
                core[0] == 0, own[n, :, pl.ds(at, width)], sib[n, :, g * width : (g + 1) * width]
            )

        def vectors(n):
            if n >= half:
                return vec_p[n - half]
            return jnp.where(core[0] == 0, vec[n], vec_s[n])

        one_group(listed, rounds, w, g * width, slabs, vectors, out, prod, total, fresh and g == start)


def last_kernel(core, own, sib, s2, near, far, give, keep):
    half, pairs, _ = own.shape
    half_g, trials = s2.shape
    width = 256
    own_at = core[0] * half_g

    def exchange(slab):
        acc = jnp.zeros((half * pairs, trials), F32)
        for g in range(half_g // width):
            flat = slab(g).reshape(half * pairs, width)
            acc += jnp.dot(flat, s2[g * width : (g + 1) * width], preferred_element_type=F32)
        return acc.reshape(half, pairs, trials)

    mine = exchange(lambda g: own[:, :, pl.ds(pl.multiple_of(own_at + g * width, width), width)]) - near[:half]
    other = exchange(lambda g: sib[:, :, g * width : (g + 1) * width]) - near[half:]

    @pl.when(core[0] == 0)
    def _():
        keep[:half] = mine - far[:half]
        keep[half:] = other
        give[:half] = (-far[half:]).astype(BF16)
        give[half:] = other.astype(BF16)

    @pl.when(core[0] != 0)
    def _():
        keep[:half] = -far[half:]
        keep[half:] = mine
        give[:half] = (other - far[:half]).astype(BF16)
        give[half:] = mine.astype(BF16)


def density_steps(part, me, size):
    rows = part.shape[0] // 2
    high = (me // 2) % 2
    keep = lax.dynamic_slice_in_dim(part, high * rows, rows, 0)
    part = keep + (yield lax.dynamic_slice_in_dim(part, (1 - high) * rows, rows, 0).astype(BF16), 2).astype(F32)
    bit = 4
    while bit < size:
        part = part + (yield part.astype(BF16), bit).astype(F32)
        bit *= 2
    part = part.astype(BF16)
    other = yield part, 2
    return jnp.where(high == 0, jnp.concatenate([part, other], 0), jnp.concatenate([other, part], 0))


class Density:
    def __init__(self, steps, size):
        self.steps, self.size, self.result = steps, size, None
        self.send(None)

    def send(self, got):
        try:
            self.give, self.bit = self.steps.send(got)
        except StopIteration as stop:
            self.give, self.result = stop.value, stop.value

    def after(self, value):
        if self.result is None:
            came = lax.ppermute(self.give, "ka", [(i, i ^ self.bit) for i in range(self.size)])
            came, value = lax.optimization_barrier((came, value))
            self.send(came)
        return self.before(value)

    def before(self, value):
        self.give, value = lax.optimization_barrier((self.give, value))
        return value

    def finish(self):
        while self.result is None:
            self.after(jnp.zeros((1,), F32))
        return self.give


def on_device(pair_density, trial_vectors, energy, coulomb, screen, neighbors, live_count, q_index):
    local_k, pair_count, local_g = pair_density.shape
    trial_count = trial_vectors.shape[2]
    q_count, _, width = screen.shape
    slots = neighbors.shape[1]
    size, parts = lax.axis_size("ka"), lax.axis_size("ga")
    me, mine = lax.axis_index("ka"), lax.axis_index("ga")
    core = me % 2
    core_id = core.astype(jnp.int32)[None]
    half_g = local_g // 2
    groups = half_g // width
    sibling = [(i, i ^ 1) for i in range(size)]
    onward = [(i, (i + 2) % size) for i in range(size)]
    to_next = [[(i, (i + 1 + target) % size) for i in range(1, size, 2)] for target in range(2)]

    def pick(first, second):
        return jnp.where(core == 0, first, second)

    offset = (neighbors // local_k - me + 1) % size
    table = jnp.concatenate([offset * local_k + neighbors % local_k, q_index, live_count[:, None]], axis=1)
    table_s = lax.ppermute(table, "ka", sibling)
    vec_s = lax.ppermute(trial_vectors, "ka", sibling)
    edge = (pick(table_s, table), pick(vec_s, trial_vectors))
    table_p, vec_p = (lax.ppermute(value, "ka", onward) for value in edge)

    def packed(core_id, last, count):
        return pl.pallas_call(
            pack_kernel,
            out_shape=[jax.ShapeDtypeStruct((local_k, pair_count, last), BF16)] * count,
            in_specs=[IN_SMEM, ANYWHERE],
            out_specs=[ANYWHERE] * count,
            scratch_shapes=[pltpu.SemaphoreType.DMA((count,))],
        )(core_id, pair_density)

    (give_half,) = packed(core_id, half_g, 1)
    first_pieces = packed(lax.optimization_barrier((core_id, *edge))[0], width, 2)
    sib = lax.ppermute(give_half, "ka", sibling)
    own_half = lax.dynamic_slice_in_dim(pair_density, core * half_g, half_g, 2)
    came = [[lax.ppermute(piece, "ka", pairs) for piece, pairs in zip(first_pieces, to_next)]]

    def send_group(g, value):
        piece = pick(sib[:, :, g * width : (g + 1) * width], own_half[:, :, g * width : (g + 1) * width])
        piece, value = lax.optimization_barrier((piece, value))
        came.append([lax.ppermute(piece, "ka", onward)])
        piece, value = lax.optimization_barrier((piece, value))
        return value

    contract = lambda v, d: lax.dot_general(d, v, (((0, 1), (0, 1)), ((), ())), preferred_element_type=F32)
    part = contract(trial_vectors, own_half) + contract(vec_s, sib)
    density = Density(density_steps(part, me, size), size)
    my_coulomb = lax.dynamic_slice_in_dim(coulomb, core * half_g, half_g, 0)

    def columns(t):
        live = jnp.arange(slots, dtype=jnp.int32)[None, :] < t[:, 2 * slots :]
        near = t[:, :slots]
        return near // local_k, near % local_k, t[:, slots : 2 * slots], live

    row = jnp.broadcast_to(jnp.arange(local_k, dtype=jnp.int32)[:, None], (local_k, slots))
    flat = lambda u, v: jnp.concatenate([u.reshape(-1), v.reshape(-1)])
    length = 2 * local_k * slots + q_count
    length = (length + UNROLL - 1) // UNROLL * UNROLL

    def listing(u, v, u_slot, v_slot, u_valid, v_valid):
        return pair_list(
            flat(u_slot, v_slot),
            flat(row, row + local_k),
            flat(u[2], v[2]),
            flat(u[3] & u_valid, v[3] & v_valid),
            q_count,
            length,
            2 * local_k,
        )

    own_t, sib_t = columns(table), columns(table_s)
    own_cross, sib_cross = own_t[0] == 2 - 2 * core, sib_t[0] == 2 * core
    near_list, near_rounds = listing(
        own_t,
        sib_t,
        own_t[1] + local_k * own_cross,
        sib_t[1] + local_k * (sib_t[0] == 1),
        own_cross | (own_t[0] == 1),
        sib_cross | (sib_t[0] == 1),
    )
    a_t, p_t = columns(pick(table, table_s)), columns(table_p)
    far_list, far_rounds = listing(a_t, p_t, a_t[1] + local_k, p_t[1], a_t[0] == 0, p_t[0] == 2)

    sums = jax.ShapeDtypeStruct((2 * local_k, pair_count, trial_count), F32)
    work = [
        VMEM((2 * local_k, trial_count, width), BF16),
        VMEM((2 * local_k + 1, trial_count, width), F32),
    ]

    def params():
        return pltpu.CompilerParams(vmem_limit_bytes=20 << 20)

    def cost(count, pairs):
        return pl.CostEstimate(
            flops=4 * count * pairs * width * width * trial_count, transcendentals=0, bytes_accessed=1 << 20
        )

    near_groups = (groups + 1) // 2
    near_rounds, vec_p, far_list, far_rounds = lax.optimization_barrier(
        (near_rounds, vec_p, far_list, far_rounds)
    )
    near_rounds = density.before(near_rounds)
    if groups > 1:
        near_rounds = send_group(1, near_rounds)
    near, w_half = pl.pallas_call(
        functools.partial(near_kernel, 0, near_groups, True),
        out_shape=(sums, jax.ShapeDtypeStruct((q_count, half_g, width), BF16)),
        in_specs=[IN_SMEM] * 3 + [IN_VMEM] * 4 + [ANYWHERE],
        out_specs=(IN_VMEM, IN_VMEM),
        scratch_shapes=work + [pltpu.SemaphoreType.DMA((groups,))],
        compiler_params=params(),
        cost_estimate=cost(near_groups, 160),
    )(core_id, near_list, near_rounds, pair_density, trial_vectors, sib, vec_s, screen)
    near = density.after(near)
    if groups > 2:
        near = send_group(2, near)
    if groups > near_groups:
        near = pl.pallas_call(
            functools.partial(near_kernel, near_groups, groups - near_groups, False),
            out_shape=sums,
            in_specs=[IN_SMEM] * 3 + [IN_VMEM] * 6,
            out_specs=IN_VMEM,
            scratch_shapes=work,
            input_output_aliases={8: 0},
            compiler_params=params(),
            cost_estimate=cost(groups - near_groups, 160),
        )(core_id, near_list, near_rounds, pair_density, trial_vectors, sib, vec_s, w_half, near)
        near = density.after(near)
    for g in range(3, groups):
        near = send_group(g, near)
    near, far_rounds = lax.optimization_barrier((near, far_rounds))
    far = None
    for c in range(groups):
        far = pl.pallas_call(
            functools.partial(far_kernel, c, 1, c == 0, len(came[c])),
            out_shape=sums,
            in_specs=[IN_SMEM] * 3 + [IN_VMEM] * (6 + (c > 0)) + [ANYWHERE] * len(came[c]),
            out_specs=IN_VMEM,
            scratch_shapes=work
            + [VMEM((local_k, pair_count, width), BF16), pltpu.SemaphoreType.DMA],
            input_output_aliases={9: 0} if c else {},
            compiler_params=params(),
            cost_estimate=cost(1, 80),
        )(
            core_id, far_list, far_rounds, pair_density, trial_vectors, sib, vec_s, w_half, vec_p,
            *([far] if c else []), *came[c],
        )
        if c % 2 == 1:
            far = density.after(far)
    screened2 = (2.0 * my_coulomb[:, None] * density.finish().astype(F32)).astype(BF16)
    give, keep = pl.pallas_call(
        last_kernel,
        out_shape=(jax.ShapeDtypeStruct(sums.shape, BF16), sums),
        in_specs=[IN_SMEM] + [IN_VMEM] * 5,
        out_specs=(IN_VMEM, IN_VMEM),
        compiler_params=params(),
        cost_estimate=cost(1, 16),
    )(core_id, pair_density, sib, screened2, near, far)

    both = keep + lax.ppermute(give, "ka", sibling).astype(F32)
    edge, inner = both[:local_k], both[local_k:]
    rows = pair_count // parts
    rows_of = lambda value, at: lax.dynamic_slice_in_dim(value, at * rows, rows, 1)
    stay = lambda first: [(i, i) for i in range(first, size, 2)]
    back = [(i, (i - 2) % size) for i in range(1, size, 2)]

    def sent(value, steps, ka_pairs):
        pairs = [
            (s * parts + g, d * parts + (g + steps) % parts) for s, d in ka_pairs for g in range(parts)
        ]
        return lax.ppermute(
            rows_of(value, (mine + steps) % parts).astype(BF16), ("ka", "ga"), pairs
        ).astype(F32)

    answer = jnp.where(core == 0, rows_of(edge, mine), rows_of(inner, mine))
    answer = answer + sent(edge, 0, back)
    for steps in range(1, parts):
        answer = answer + sent(edge, steps, stay(0) + back) + sent(inner, steps, stay(1))
    energy_rows = lax.dynamic_slice_in_dim(energy, mine * rows, rows, 1)
    vector_rows = lax.dynamic_slice_in_dim(trial_vectors, mine * rows, rows, 1)
    return (energy_rows[:, :, None] * vector_rows.astype(F32) + answer).astype(BF16)


def solution(mesh):
    in_specs = (
        P("ka", None, "ga"),
        P("ka", None, None),
        P("ka", None),
        P("ga"),
        P(None, "ga", None),
        P("ka", None),
        P("ka"),
        P("ka", None),
    )
    out_specs = P("ka", "ga", None)
    return jax.shard_map(
        on_device, mesh=mesh, in_specs=in_specs, out_specs=out_specs, check_vma=False
    )
```

```python
import functools

import jax
import jax.numpy as jnp
from jax import lax
from jax.experimental import pallas as pl
from jax.experimental.pallas import tpu as pltpu
from jax.sharding import PartitionSpec as P

UNROLL = 32
F32, BF16 = jnp.float32, jnp.bfloat16
VMEM, SMEM = pltpu.VMEM, pltpu.SMEM
IN_VMEM, IN_SMEM, ANYWHERE = (pl.BlockSpec(memory_space=space) for space in (VMEM, SMEM, pl.ANY))


def pair_list(n_slot, k_slot, q, valid, q_count, length, spare):
    entries = q.shape[0]
    order = jnp.arange(entries, dtype=jnp.int32)
    qs = jnp.arange(q_count, dtype=jnp.int32)
    same = (q[:, None] == q[None, :]) & valid[None, :] & (order[None, :] < order[:, None])
    within = jnp.sum(same.astype(jnp.int32), axis=1)
    count = jnp.sum(((q[None, :] == qs[:, None]) & valid[None, :]).astype(jnp.int32), axis=1)
    padded = (count + 1) // 2 * 2
    base = jnp.sum(jnp.where(qs[None, :] < q[:, None], padded[None, :], 0), axis=1)
    place = jnp.where(valid, base + within, -1)
    code = n_slot + 64 * k_slot + 4096 * q
    blank = 64 * spare
    rows = jnp.arange(length, dtype=jnp.int32)
    listed = blank + jnp.sum(jnp.where(place[None, :] == rows[:, None], code[None, :] - blank, 0), axis=1)
    rounds = (jnp.sum(padded) + UNROLL - 1) // UNROLL
    return listed, rounds[None]


def dot_last(u, v):
    return lax.dot_general(u, v, (((1,), (1,)), ((), ())), preferred_element_type=F32)


def one_group(listed, rounds, w_ref, row, slabs, vectors, out_ref, prod, total, first):
    trials = prod.shape[1]
    width = prod.shape[2]
    slots = prod.shape[0]

    for n in range(slots):
        made = lax.dot_general(vectors(n), slabs(n), (((0,), (0,)), ((), ())), preferred_element_type=F32)
        prod[n] = made.astype(BF16)
    total[...] = jnp.zeros_like(total)

    def some(i, _):
        for d in range(0, UNROLL, 2):
            a, b = listed[i * UNROLL + d], listed[i * UNROLL + d + 1]
            both = jnp.concatenate([prod[a & 63], prod[b & 63]], axis=0)
            made = dot_last(both, w_ref[a >> 12, pl.ds(row, width), :])
            total[(a >> 6) & 63] += made[:trials]
            total[(b >> 6) & 63] += made[trials:]
        return 0

    lax.fori_loop(0, rounds[0], some, 0)
    for k in range(slots):
        made = dot_last(slabs(k), total[k].astype(BF16))

        if first:
            out_ref[k] = made
        else:
            out_ref[k] += made


def pack_kernel(core, source, *refs):
    outs, sems = refs[:-1], refs[-1]
    half_g, size = source.shape[2] // 2, outs[0].shape[2]
    if len(outs) == 1:
        starts = [pl.multiple_of((1 - core[0]) * half_g, size)]
    else:
        starts = [0, half_g]
    copies = [
        pltpu.make_async_copy(source.at[:, :, pl.ds(start, size)], out, sems.at[i])
        for i, (start, out) in enumerate(zip(starts, outs))
    ]
    for copy in copies:
        copy.start()
    for copy in copies:
        copy.wait()


def near_kernel(start, count, load, *refs):
    if load:
        core, listed, rounds, own, vec, sib, vec_s, screen, out, w, prod, total, sems = refs
    else:
        core, listed, rounds, own, vec, sib, vec_s, w, _, out, prod, total = refs
    half, _, _ = own.shape
    width = prod.shape[2]
    half_g = w.shape[1]
    groups = half_g // width
    own_at = core[0] * half_g

    def copy(g):
        return pltpu.make_async_copy(
            screen.at[:, pl.ds(pl.multiple_of(own_at + g * width, width), width), :],
            w.at[:, pl.ds(g * width, width), :],
            sems.at[g],
        )

    if load:
        for g in range(groups):
            copy(g).start()
    for g in range(start, start + count):
        if load:
            copy(g).wait()
        at = pl.multiple_of(own_at + g * width, width)

        def slabs(n, at=at, g=g):
            return own[n, :, pl.ds(at, width)] if n < half else sib[n - half, :, g * width : (g + 1) * width]

        def vectors(n):
            return vec[n] if n < half else vec_s[n - half]

        one_group(listed, rounds, w, g * width, slabs, vectors, out, prod, total, load and g == start)
    if load:
        for g in range(start + count, groups):
            copy(g).wait()


def far_kernel(start, count, fresh, sources, core, listed, rounds, own, vec, sib, vec_s, w, vec_p, *refs):
    refs = refs[0 if fresh else 1 :]
    sources, (out, prod, total, came, sem) = refs[:sources], refs[sources:]
    half, _, _ = own.shape
    width = prod.shape[2]
    half_g = w.shape[1]
    own_at = core[0] * half_g
    if len(sources) == 1:
        pltpu.make_async_copy(sources[0], came, sem).start()
    else:

        @pl.when(core[0] == 0)
        def _():
            pltpu.make_async_copy(sources[0], came, sem).start()

        @pl.when(core[0] != 0)
        def _():
            pltpu.make_async_copy(sources[1], came, sem).start()

    pltpu.make_async_copy(sources[0], came, sem).wait()
    for g in range(start, start + count):
        at = pl.multiple_of(own_at + g * width, width)

        def slabs(n, at=at, g=g):
            if n >= half:
                return came[n - half, :, (g - start) * width : (g - start + 1) * width]
            return jnp.where(
                core[0] == 0, own[n, :, pl.ds(at, width)], sib[n, :, g * width : (g + 1) * width]
            )

        def vectors(n):
            if n >= half:
                return vec_p[n - half]
            return jnp.where(core[0] == 0, vec[n], vec_s[n])

        one_group(listed, rounds, w, g * width, slabs, vectors, out, prod, total, fresh and g == start)


def last_kernel(core, own, sib, s2, near, far, give, keep):
    half, pairs, _ = own.shape
    trials, half_g = s2.shape
    width = 256
    own_at = core[0] * half_g

    def exchange(slab):
        acc = jnp.zeros((half * pairs, trials), F32)
        for g in range(half_g // width):
            acc += dot_last(slab(g).reshape(half * pairs, width), s2[:, g * width : (g + 1) * width])
        return acc.reshape(half, pairs, trials)

    mine = exchange(lambda g: own[:, :, pl.ds(pl.multiple_of(own_at + g * width, width), width)]) - near[:half]
    other = exchange(lambda g: sib[:, :, g * width : (g + 1) * width]) - near[half:]

    @pl.when(core[0] == 0)
    def _():
        keep[:half] = mine - far[:half]
        keep[half:] = other
        give[:half] = (-far[half:]).astype(BF16)
        give[half:] = other.astype(BF16)

    @pl.when(core[0] != 0)
    def _():
        keep[:half] = -far[half:]
        keep[half:] = mine
        give[:half] = (other - far[:half]).astype(BF16)
        give[half:] = mine.astype(BF16)


def density_steps(part, me, size):
    columns = part.shape[1] // 2
    high = (me // 2) % 2
    keep = lax.dynamic_slice_in_dim(part, high * columns, columns, 1)
    give = lax.dynamic_slice_in_dim(part, (1 - high) * columns, columns, 1).astype(BF16)
    part = keep + (yield give, 2).astype(F32)
    bit = 4
    while bit < size:
        part = part + (yield part.astype(BF16), bit).astype(F32)
        bit *= 2
    part = part.astype(BF16)
    other = yield part, 2
    return jnp.where(high == 0, jnp.concatenate([part, other], 1), jnp.concatenate([other, part], 1))


class Density:
    def __init__(self, steps, size):
        self.steps, self.size, self.result = steps, size, None
        self.send(None)

    def send(self, got):
        try:
            self.give, self.bit = self.steps.send(got)
        except StopIteration as stop:
            self.give, self.result = stop.value, stop.value

    def after(self, value):
        if self.result is None:
            came = lax.ppermute(self.give, "ka", [(i, i ^ self.bit) for i in range(self.size)])
            came, value = lax.optimization_barrier((came, value))
            self.send(came)
        return self.before(value)

    def before(self, value):
        self.give, value = lax.optimization_barrier((self.give, value))
        return value

    def finish(self):
        while self.result is None:
            self.after(jnp.zeros((1,), F32))
        return self.give


def on_device(pair_density, trial_vectors, energy, coulomb, screen, neighbors, live_count, q_index):
    local_k, pair_count, local_g = pair_density.shape
    trial_count = trial_vectors.shape[2]
    q_count, _, width = screen.shape
    slots = neighbors.shape[1]
    size, parts = lax.axis_size("ka"), lax.axis_size("ga")
    me, mine = lax.axis_index("ka"), lax.axis_index("ga")
    core = me % 2
    core_id = core.astype(jnp.int32)[None]
    half_g = local_g // 2
    groups = half_g // width
    sibling = [(i, i ^ 1) for i in range(size)]
    onward = [(i, (i + 2) % size) for i in range(size)]
    to_next = [[(i, (i + 1 + target) % size) for i in range(1, size, 2)] for target in range(2)]

    def pick(first, second):
        return jnp.where(core == 0, first, second)

    offset = (neighbors // local_k - me + 1) % size
    table = jnp.concatenate([offset * local_k + neighbors % local_k, q_index, live_count[:, None]], axis=1)
    table_s = lax.ppermute(table, "ka", sibling)
    vec_s = lax.ppermute(trial_vectors, "ka", sibling)
    edge = (pick(table_s, table), pick(vec_s, trial_vectors))
    table_p, vec_p = (lax.ppermute(value, "ka", onward) for value in edge)

    def packed(core_id, last, count):
        return pl.pallas_call(
            pack_kernel,
            out_shape=[jax.ShapeDtypeStruct((local_k, pair_count, last), BF16)] * count,
            in_specs=[IN_SMEM, ANYWHERE],
            out_specs=[IN_VMEM] * count,
            scratch_shapes=[pltpu.SemaphoreType.DMA((count,))],
        )(core_id, pair_density)

    (give_half,) = packed(core_id, half_g, 1)
    first_pieces = packed(lax.optimization_barrier((core_id, *edge))[0], width, 2)
    sib = lax.ppermute(give_half, "ka", sibling)
    own_half = lax.dynamic_slice_in_dim(pair_density, core * half_g, half_g, 2)
    came = [[lax.ppermute(piece, "ka", pairs) for piece, pairs in zip(first_pieces, to_next)]]

    def send_group(g, value):
        piece = pick(sib[:, :, g * width : (g + 1) * width], own_half[:, :, g * width : (g + 1) * width])
        piece, value = lax.optimization_barrier((piece, value))
        came.append([lax.ppermute(piece, "ka", onward)])
        piece, value = lax.optimization_barrier((piece, value))
        return value

    contract = lambda v, d: lax.dot_general(v, d, (((0, 1), (0, 1)), ((), ())), preferred_element_type=F32)
    part = contract(trial_vectors, own_half) + contract(vec_s, sib)
    density = Density(density_steps(part, me, size), size)
    my_coulomb = lax.dynamic_slice_in_dim(coulomb, core * half_g, half_g, 0)

    def columns(t):
        live = jnp.arange(slots, dtype=jnp.int32)[None, :] < t[:, 2 * slots :]
        near = t[:, :slots]
        return near // local_k, near % local_k, t[:, slots : 2 * slots], live

    row = jnp.broadcast_to(jnp.arange(local_k, dtype=jnp.int32)[:, None], (local_k, slots))
    flat = lambda u, v: jnp.concatenate([u.reshape(-1), v.reshape(-1)])
    length = 2 * local_k * slots + q_count
    length = (length + UNROLL - 1) // UNROLL * UNROLL

    def listing(u, v, u_slot, v_slot, u_valid, v_valid):
        return pair_list(
            flat(u_slot, v_slot),
            flat(row, row + local_k),
            flat(u[2], v[2]),
            flat(u[3] & u_valid, v[3] & v_valid),
            q_count,
            length,
            2 * local_k,
        )

    own_t, sib_t = columns(table), columns(table_s)
    own_cross, sib_cross = own_t[0] == 2 - 2 * core, sib_t[0] == 2 * core
    near_list, near_rounds = listing(
        own_t,
        sib_t,
        own_t[1] + local_k * own_cross,
        sib_t[1] + local_k * (sib_t[0] == 1),
        own_cross | (own_t[0] == 1),
        sib_cross | (sib_t[0] == 1),
    )
    a_t, p_t = columns(pick(table, table_s)), columns(table_p)
    far_list, far_rounds = listing(a_t, p_t, a_t[1] + local_k, p_t[1], a_t[0] == 0, p_t[0] == 2)

    sums = jax.ShapeDtypeStruct((2 * local_k, pair_count, trial_count), F32)
    work = [
        VMEM((2 * local_k, trial_count, width), BF16),
        VMEM((2 * local_k + 1, trial_count, width), F32),
    ]

    def params():
        return pltpu.CompilerParams(vmem_limit_bytes=12 << 20)

    def cost(count, pairs):
        return pl.CostEstimate(
            flops=4 * count * pairs * width * width * trial_count, transcendentals=0, bytes_accessed=1 << 20
        )

    near_rounds, vec_p, far_list, far_rounds = lax.optimization_barrier(
        (near_rounds, vec_p, far_list, far_rounds)
    )
    near_rounds = density.before(near_rounds)
    near, w_half = pl.pallas_call(
        functools.partial(near_kernel, 0, 1, True),
        out_shape=(sums, jax.ShapeDtypeStruct((q_count, half_g, width), BF16)),
        in_specs=[IN_SMEM] * 3 + [IN_VMEM] * 4 + [ANYWHERE],
        out_specs=(IN_VMEM, IN_VMEM),
        scratch_shapes=work + [pltpu.SemaphoreType.DMA((groups,))],
        compiler_params=params(),
        cost_estimate=cost(1, 160),
    )(core_id, near_list, near_rounds, pair_density, trial_vectors, sib, vec_s, screen)
    near = density.after(near)
    for start, count, going in ((1, 1, (1,)), (2, groups - 2, range(2, groups))):
        if count < 1 or start >= groups:
            continue
        for g in going:
            near = send_group(g, near)
        near = pl.pallas_call(
            functools.partial(near_kernel, start, count, False),
            out_shape=sums,
            in_specs=[IN_SMEM] * 3 + [IN_VMEM] * 6,
            out_specs=IN_VMEM,
            scratch_shapes=work,
            input_output_aliases={8: 0},
            compiler_params=params(),
            cost_estimate=cost(count, 160),
        )(core_id, near_list, near_rounds, pair_density, trial_vectors, sib, vec_s, w_half, near)
        near = density.after(near)
    near, far_rounds = lax.optimization_barrier((near, far_rounds))
    far = None
    for c in range(groups):
        far = pl.pallas_call(
            functools.partial(far_kernel, c, 1, c == 0, len(came[c])),
            out_shape=sums,
            in_specs=[IN_SMEM] * 3 + [IN_VMEM] * (6 + (c > 0)) + [ANYWHERE] * len(came[c]),
            out_specs=IN_VMEM,
            scratch_shapes=work
            + [VMEM((local_k, pair_count, width), BF16), pltpu.SemaphoreType.DMA],
            input_output_aliases={9: 0} if c else {},
            compiler_params=params(),
            cost_estimate=cost(1, 80),
        )(
            core_id, far_list, far_rounds, pair_density, trial_vectors, sib, vec_s, w_half, vec_p,
            *([far] if c else []), *came[c],
        )
        if c % 2 == 1:
            far = density.after(far)
    screened2 = (2.0 * my_coulomb[None, :] * density.finish().astype(F32)).astype(BF16)
    give, keep = pl.pallas_call(
        last_kernel,
        out_shape=(jax.ShapeDtypeStruct(sums.shape, BF16), sums),
        in_specs=[IN_SMEM] + [IN_VMEM] * 5,
        out_specs=(IN_VMEM, IN_VMEM),
        compiler_params=params(),
        cost_estimate=cost(1, 16),
    )(core_id, pair_density, sib, screened2, near, far)

    both = keep + lax.ppermute(give, "ka", sibling).astype(F32)
    edge, inner = both[:local_k], both[local_k:]
    rows = pair_count // parts
    rows_of = lambda value, at: lax.dynamic_slice_in_dim(value, at * rows, rows, 1)
    stay = lambda first: [(i, i) for i in range(first, size, 2)]
    back = [(i, (i - 2) % size) for i in range(1, size, 2)]

    def sent(value, steps, ka_pairs):
        pairs = [
            (s * parts + g, d * parts + (g + steps) % parts) for s, d in ka_pairs for g in range(parts)
        ]
        return lax.ppermute(
            rows_of(value, (mine + steps) % parts).astype(BF16), ("ka", "ga"), pairs
        ).astype(F32)

    answer = jnp.where(core == 0, rows_of(edge, mine), rows_of(inner, mine))
    answer = answer + sent(edge, 0, back)
    for steps in range(1, parts):
        answer = answer + sent(edge, steps, stay(0) + back) + sent(inner, steps, stay(1))
    energy_rows = lax.dynamic_slice_in_dim(energy, mine * rows, rows, 1)
    vector_rows = lax.dynamic_slice_in_dim(trial_vectors, mine * rows, rows, 1)
    return (energy_rows[:, :, None] * vector_rows.astype(F32) + answer).astype(BF16)


def solution(mesh):
    in_specs = (
        P("ka", None, "ga"),
        P("ka", None, None),
        P("ka", None),
        P("ga"),
        P(None, "ga", None),
        P("ka", None),
        P("ka"),
        P("ka", None),
    )
    out_specs = P("ka", "ga", None)
    return jax.shard_map(
        on_device, mesh=mesh, in_specs=in_specs, out_specs=out_specs, check_vma=False
    )
```

```python
import functools

import jax
import jax.numpy as jnp
from jax import lax
from jax.experimental import pallas as pl
from jax.experimental.pallas import tpu as pltpu
from jax.sharding import PartitionSpec as P

UNROLL = 32
F32, BF16 = jnp.float32, jnp.bfloat16
VMEM, SMEM = pltpu.VMEM, pltpu.SMEM
IN_VMEM, IN_SMEM, ANYWHERE = (pl.BlockSpec(memory_space=space) for space in (VMEM, SMEM, pl.ANY))


def pair_list(n_slot, k_slot, q, valid, q_count, length, spare):
    entries = q.shape[0]
    order = jnp.arange(entries, dtype=jnp.int32)
    qs = jnp.arange(q_count, dtype=jnp.int32)
    same = (q[:, None] == q[None, :]) & valid[None, :] & (order[None, :] < order[:, None])
    within = jnp.sum(same.astype(jnp.int32), axis=1)
    count = jnp.sum(((q[None, :] == qs[:, None]) & valid[None, :]).astype(jnp.int32), axis=1)
    padded = (count + 1) // 2 * 2
    base = jnp.sum(jnp.where(qs[None, :] < q[:, None], padded[None, :], 0), axis=1)
    place = jnp.where(valid, base + within, -1)
    code = n_slot + 64 * k_slot + 4096 * q
    blank = 64 * spare
    rows = jnp.arange(length, dtype=jnp.int32)
    listed = blank + jnp.sum(jnp.where(place[None, :] == rows[:, None], code[None, :] - blank, 0), axis=1)
    rounds = (jnp.sum(padded) + UNROLL - 1) // UNROLL
    return listed, rounds[None]


def dot_last(u, v):
    return lax.dot_general(u, v, (((1,), (1,)), ((), ())), preferred_element_type=F32)


def one_group(listed, rounds, w_ref, row, slabs, vectors, out_ref, prod, total, first):
    trials = prod.shape[1]
    width = prod.shape[2]
    slots = prod.shape[0]

    for n in range(slots):
        made = lax.dot_general(vectors(n), slabs(n), (((0,), (0,)), ((), ())), preferred_element_type=F32)
        prod[n] = made.astype(BF16)
    total[...] = jnp.zeros_like(total)

    def some(i, _):
        for d in range(0, UNROLL, 2):
            a, b = listed[i * UNROLL + d], listed[i * UNROLL + d + 1]
            both = jnp.concatenate([prod[a & 63], prod[b & 63]], axis=0)
            made = dot_last(both, w_ref[a >> 12, pl.ds(row, width), :])
            total[(a >> 6) & 63] += made[:trials]
            total[(b >> 6) & 63] += made[trials:]
        return 0

    lax.fori_loop(0, rounds[0], some, 0)
    for k in range(slots):
        made = dot_last(slabs(k), total[k].astype(BF16))

        if first:
            out_ref[k] = made
        else:
            out_ref[k] += made


def pack_kernel(core, source, *refs):
    outs, sems = refs[:-1], refs[-1]
    half_g, size = source.shape[2] // 2, outs[0].shape[2]
    if len(outs) == 1:
        starts = [pl.multiple_of((1 - core[0]) * half_g, size)]
    else:
        starts = [0, half_g]
    copies = [
        pltpu.make_async_copy(source.at[:, :, pl.ds(start, size)], out, sems.at[i])
        for i, (start, out) in enumerate(zip(starts, outs))
    ]
    for copy in copies:
        copy.start()
    for copy in copies:
        copy.wait()


def near_kernel(start, count, load, *refs):
    if load:
        core, listed, rounds, own, vec, sib, vec_s, screen, out, w, prod, total, sems = refs
    else:
        core, listed, rounds, own, vec, sib, vec_s, w, _, out, prod, total = refs
    half, _, _ = own.shape
    width = prod.shape[2]
    half_g = w.shape[1]
    groups = half_g // width
    own_at = core[0] * half_g

    def copy(g):
        return pltpu.make_async_copy(
            screen.at[:, pl.ds(pl.multiple_of(own_at + g * width, width), width), :],
            w.at[:, pl.ds(g * width, width), :],
            sems.at[g],
        )

    if load:
        for g in range(groups):
            copy(g).start()
    for g in range(start, start + count):
        if load:
            copy(g).wait()
        at = pl.multiple_of(own_at + g * width, width)

        def slabs(n, at=at, g=g):
            return own[n, :, pl.ds(at, width)] if n < half else sib[n - half, :, g * width : (g + 1) * width]

        def vectors(n):
            return vec[n] if n < half else vec_s[n - half]

        one_group(listed, rounds, w, g * width, slabs, vectors, out, prod, total, load and g == start)
    if load:
        for g in range(start + count, groups):
            copy(g).wait()


def far_kernel(start, count, fresh, sources, core, listed, rounds, own, vec, sib, vec_s, w, vec_p, *refs):
    refs = refs[0 if fresh else 1 :]
    sources, (out, prod, total, came, sem) = refs[:sources], refs[sources:]
    half, _, _ = own.shape
    width = prod.shape[2]
    half_g = w.shape[1]
    own_at = core[0] * half_g
    if len(sources) == 1:
        pltpu.make_async_copy(sources[0], came, sem).start()
    else:

        @pl.when(core[0] == 0)
        def _():
            pltpu.make_async_copy(sources[0], came, sem).start()

        @pl.when(core[0] != 0)
        def _():
            pltpu.make_async_copy(sources[1], came, sem).start()

    pltpu.make_async_copy(sources[0], came, sem).wait()
    for g in range(start, start + count):
        at = pl.multiple_of(own_at + g * width, width)

        def slabs(n, at=at, g=g):
            if n >= half:
                return came[n - half, :, (g - start) * width : (g - start + 1) * width]
            return jnp.where(
                core[0] == 0, own[n, :, pl.ds(at, width)], sib[n, :, g * width : (g + 1) * width]
            )

        def vectors(n):
            if n >= half:
                return vec_p[n - half]
            return jnp.where(core[0] == 0, vec[n], vec_s[n])

        one_group(listed, rounds, w, g * width, slabs, vectors, out, prod, total, fresh and g == start)


def last_kernel(core, own, sib, s2, near, far, give, keep):
    half, pairs, _ = own.shape
    trials, half_g = s2.shape
    width = 256
    own_at = core[0] * half_g

    def exchange(slab):
        acc = jnp.zeros((half * pairs, trials), F32)
        for g in range(half_g // width):
            acc += dot_last(slab(g).reshape(half * pairs, width), s2[:, g * width : (g + 1) * width])
        return acc.reshape(half, pairs, trials)

    mine = exchange(lambda g: own[:, :, pl.ds(pl.multiple_of(own_at + g * width, width), width)]) - near[:half]
    other = exchange(lambda g: sib[:, :, g * width : (g + 1) * width]) - near[half:]

    @pl.when(core[0] == 0)
    def _():
        keep[:half] = mine - far[:half]
        keep[half:] = other
        give[:half] = (-far[half:]).astype(BF16)
        give[half:] = other.astype(BF16)

    @pl.when(core[0] != 0)
    def _():
        keep[:half] = -far[half:]
        keep[half:] = mine
        give[:half] = (other - far[:half]).astype(BF16)
        give[half:] = mine.astype(BF16)


def density_steps(part, me, size):
    columns = part.shape[1] // 2
    high = (me // 2) % 2
    keep = lax.dynamic_slice_in_dim(part, high * columns, columns, 1)
    give = lax.dynamic_slice_in_dim(part, (1 - high) * columns, columns, 1).astype(BF16)
    part = keep + (yield give, 2).astype(F32)
    bit = 4
    while bit < size:
        part = part + (yield part.astype(BF16), bit).astype(F32)
        bit *= 2
    part = part.astype(BF16)
    other = yield part, 2
    return jnp.where(high == 0, jnp.concatenate([part, other], 1), jnp.concatenate([other, part], 1))


class Density:
    def __init__(self, steps, size):
        self.steps, self.size, self.result = steps, size, None
        self.send(None)

    def send(self, got):
        try:
            self.give, self.bit = self.steps.send(got)
        except StopIteration as stop:
            self.give, self.result = stop.value, stop.value

    def after(self, value):
        if self.result is None:
            came = lax.ppermute(self.give, "ka", [(i, i ^ self.bit) for i in range(self.size)])
            came, value = lax.optimization_barrier((came, value))
            self.send(came)
        return self.before(value)

    def before(self, value):
        self.give, value = lax.optimization_barrier((self.give, value))
        return value

    def finish(self):
        while self.result is None:
            self.after(jnp.zeros((1,), F32))
        return self.give


def on_device(pair_density, trial_vectors, energy, coulomb, screen, neighbors, live_count, q_index):
    local_k, pair_count, local_g = pair_density.shape
    trial_count = trial_vectors.shape[2]
    q_count, _, width = screen.shape
    slots = neighbors.shape[1]
    size, parts = lax.axis_size("ka"), lax.axis_size("ga")
    me, mine = lax.axis_index("ka"), lax.axis_index("ga")
    core = me % 2
    core_id = core.astype(jnp.int32)[None]
    half_g = local_g // 2
    groups = half_g // width
    sibling = [(i, i ^ 1) for i in range(size)]
    onward = [(i, (i + 2) % size) for i in range(size)]
    to_next = [[(i, (i + 1 + target) % size) for i in range(1, size, 2)] for target in range(2)]

    def pick(first, second):
        return jnp.where(core == 0, first, second)

    offset = (neighbors // local_k - me + 1) % size
    table = jnp.concatenate([offset * local_k + neighbors % local_k, q_index, live_count[:, None]], axis=1)
    table_s = lax.ppermute(table, "ka", sibling)
    vec_s = lax.ppermute(trial_vectors, "ka", sibling)
    edge = (pick(table_s, table), pick(vec_s, trial_vectors))
    table_p, vec_p = (lax.ppermute(value, "ka", onward) for value in edge)

    def packed(core_id, last, count):
        return pl.pallas_call(
            pack_kernel,
            out_shape=[jax.ShapeDtypeStruct((local_k, pair_count, last), BF16)] * count,
            in_specs=[IN_SMEM, ANYWHERE],
            out_specs=[IN_VMEM] * count,
            scratch_shapes=[pltpu.SemaphoreType.DMA((count,))],
        )(core_id, pair_density)

    (give_half,) = packed(core_id, half_g, 1)
    first_pieces = packed(lax.optimization_barrier((core_id, edge[0]))[0], width, 2)
    sib = lax.ppermute(give_half, "ka", sibling)
    own_half = lax.dynamic_slice_in_dim(pair_density, core * half_g, half_g, 2)
    came = [[lax.ppermute(piece, "ka", pairs) for piece, pairs in zip(first_pieces, to_next)]]

    def send_group(g, value):
        piece = pick(sib[:, :, g * width : (g + 1) * width], own_half[:, :, g * width : (g + 1) * width])
        piece, value = lax.optimization_barrier((piece, value))
        came.append([lax.ppermute(piece, "ka", onward)])
        piece, value = lax.optimization_barrier((piece, value))
        return value

    contract = lambda v, d: lax.dot_general(v, d, (((0, 1), (0, 1)), ((), ())), preferred_element_type=F32)
    part = contract(trial_vectors, own_half) + contract(vec_s, sib)
    density = Density(density_steps(part, me, size), size)
    my_coulomb = lax.dynamic_slice_in_dim(coulomb, core * half_g, half_g, 0)

    def columns(t):
        live = jnp.arange(slots, dtype=jnp.int32)[None, :] < t[:, 2 * slots :]
        near = t[:, :slots]
        return near // local_k, near % local_k, t[:, slots : 2 * slots], live

    row = jnp.broadcast_to(jnp.arange(local_k, dtype=jnp.int32)[:, None], (local_k, slots))
    flat = lambda u, v: jnp.concatenate([u.reshape(-1), v.reshape(-1)])
    length = 2 * local_k * slots + q_count
    length = (length + UNROLL - 1) // UNROLL * UNROLL

    def listing(u, v, u_slot, v_slot, u_valid, v_valid):
        return pair_list(
            flat(u_slot, v_slot),
            flat(row, row + local_k),
            flat(u[2], v[2]),
            flat(u[3] & u_valid, v[3] & v_valid),
            q_count,
            length,
            2 * local_k,
        )

    own_t, sib_t = columns(table), columns(table_s)
    own_cross, sib_cross = own_t[0] == 2 - 2 * core, sib_t[0] == 2 * core
    near_list, near_rounds = listing(
        own_t,
        sib_t,
        own_t[1] + local_k * own_cross,
        sib_t[1] + local_k * (sib_t[0] == 1),
        own_cross | (own_t[0] == 1),
        sib_cross | (sib_t[0] == 1),
    )

    sums = jax.ShapeDtypeStruct((2 * local_k, pair_count, trial_count), F32)
    work = [
        VMEM((2 * local_k, trial_count, width), BF16),
        VMEM((2 * local_k + 1, trial_count, width), F32),
    ]

    def params():
        return pltpu.CompilerParams(vmem_limit_bytes=12 << 20)

    def cost(count, pairs):
        return pl.CostEstimate(
            flops=4 * count * pairs * width * width * trial_count, transcendentals=0, bytes_accessed=1 << 20
        )

    a_t, p_t = columns(pick(table, table_s)), columns(table_p)
    far_list, far_rounds = listing(a_t, p_t, a_t[1] + local_k, p_t[1], a_t[0] == 0, p_t[0] == 2)
    near_rounds, far_list, far_rounds = lax.optimization_barrier((near_rounds, far_list, far_rounds))
    near_rounds = density.before(near_rounds)
    near, w_half = pl.pallas_call(
        functools.partial(near_kernel, 0, 1, True),
        out_shape=(sums, jax.ShapeDtypeStruct((q_count, half_g, width), BF16)),
        in_specs=[IN_SMEM] * 3 + [IN_VMEM] * 4 + [ANYWHERE],
        out_specs=(IN_VMEM, IN_VMEM),
        scratch_shapes=work + [pltpu.SemaphoreType.DMA((groups,))],
        compiler_params=params(),
        cost_estimate=cost(1, 160),
    )(core_id, near_list, near_rounds, pair_density, trial_vectors, sib, vec_s, screen)
    near = density.after(near)
    near, vec_p = lax.optimization_barrier((near, vec_p))
    for start, count, going in ((1, 1, (1,)), (2, groups - 2, range(2, groups))):
        if count < 1 or start >= groups:
            continue
        if start == 2:
            near, *came[0] = lax.optimization_barrier((near, *came[0]))
        for g in going:
            near = send_group(g, near)
        near = pl.pallas_call(
            functools.partial(near_kernel, start, count, False),
            out_shape=sums,
            in_specs=[IN_SMEM] * 3 + [IN_VMEM] * 6,
            out_specs=IN_VMEM,
            scratch_shapes=work,
            input_output_aliases={8: 0},
            compiler_params=params(),
            cost_estimate=cost(count, 160),
        )(core_id, near_list, near_rounds, pair_density, trial_vectors, sib, vec_s, w_half, near)
        if start == 1:
            near = density.after(near)
    near, far_rounds = lax.optimization_barrier((near, far_rounds))
    far = None
    for c in range(groups):
        far = pl.pallas_call(
            functools.partial(far_kernel, c, 1, c == 0, len(came[c])),
            out_shape=sums,
            in_specs=[IN_SMEM] * 3 + [IN_VMEM] * (6 + (c > 0)) + [ANYWHERE] * len(came[c]),
            out_specs=IN_VMEM,
            scratch_shapes=work
            + [VMEM((local_k, pair_count, width), BF16), pltpu.SemaphoreType.DMA],
            input_output_aliases={9: 0} if c else {},
            compiler_params=params(),
            cost_estimate=cost(1, 8),
        )(
            core_id, far_list, far_rounds, pair_density, trial_vectors, sib, vec_s, w_half, vec_p,
            *([far] if c else []), *came[c],
        )
        if c in (1, groups - 1):
            far = density.after(far)
    screened2 = (2.0 * my_coulomb[None, :] * density.finish().astype(F32)).astype(BF16)
    give, keep = pl.pallas_call(
        last_kernel,
        out_shape=(jax.ShapeDtypeStruct(sums.shape, BF16), sums),
        in_specs=[IN_SMEM] + [IN_VMEM] * 5,
        out_specs=(IN_VMEM, IN_VMEM),
        compiler_params=params(),
        cost_estimate=cost(1, 16),
    )(core_id, pair_density, sib, screened2, near, far)

    both = keep + lax.ppermute(give, "ka", sibling).astype(F32)
    edge, inner = both[:local_k], both[local_k:]
    rows = pair_count // parts
    rows_of = lambda value, at: lax.dynamic_slice_in_dim(value, at * rows, rows, 1)
    stay = lambda first: [(i, i) for i in range(first, size, 2)]
    back = [(i, (i - 2) % size) for i in range(1, size, 2)]

    def sent(value, steps, ka_pairs):
        pairs = [
            (s * parts + g, d * parts + (g + steps) % parts) for s, d in ka_pairs for g in range(parts)
        ]
        return lax.ppermute(
            rows_of(value, (mine + steps) % parts).astype(BF16), ("ka", "ga"), pairs
        ).astype(F32)

    answer = jnp.where(core == 0, rows_of(edge, mine), rows_of(inner, mine))
    answer = answer + sent(edge, 0, back)
    for steps in range(1, parts):
        answer = answer + sent(edge, steps, stay(0) + back) + sent(inner, steps, stay(1))
    energy_rows = lax.dynamic_slice_in_dim(energy, mine * rows, rows, 1)
    vector_rows = lax.dynamic_slice_in_dim(trial_vectors, mine * rows, rows, 1)
    return (energy_rows[:, :, None] * vector_rows.astype(F32) + answer).astype(BF16)


def solution(mesh):
    in_specs = (
        P("ka", None, "ga"),
        P("ka", None, None),
        P("ka", None),
        P("ga"),
        P(None, "ga", None),
        P("ka", None),
        P("ka"),
        P("ka", None),
    )
    out_specs = P("ka", "ga", None)
    return jax.shard_map(
        on_device, mesh=mesh, in_specs=in_specs, out_specs=out_specs, check_vma=False
    )
```

```python
import functools

import jax
import jax.numpy as jnp
from jax import lax
from jax.experimental import pallas as pl
from jax.experimental.pallas import tpu as pltpu
from jax.sharding import PartitionSpec as P

UNROLL = 32
F32, BF16 = jnp.float32, jnp.bfloat16
VMEM, SMEM = pltpu.VMEM, pltpu.SMEM
IN_VMEM, IN_SMEM, ANYWHERE = (pl.BlockSpec(memory_space=space) for space in (VMEM, SMEM, pl.ANY))


def pair_list(n_slot, k_slot, q, valid, q_count, length, spare):
    entries = q.shape[0]
    order = jnp.arange(entries, dtype=jnp.int32)
    qs = jnp.arange(q_count, dtype=jnp.int32)
    same = (q[:, None] == q[None, :]) & valid[None, :] & (order[None, :] < order[:, None])
    within = jnp.sum(same.astype(jnp.int32), axis=1)
    count = jnp.sum(((q[None, :] == qs[:, None]) & valid[None, :]).astype(jnp.int32), axis=1)
    padded = (count + 1) // 2 * 2
    base = jnp.sum(jnp.where(qs[None, :] < q[:, None], padded[None, :], 0), axis=1)
    place = jnp.where(valid, base + within, -1)
    code = n_slot + 64 * k_slot + 4096 * q
    blank = 64 * spare
    rows = jnp.arange(length, dtype=jnp.int32)
    listed = blank + jnp.sum(jnp.where(place[None, :] == rows[:, None], code[None, :] - blank, 0), axis=1)
    rounds = (jnp.sum(padded) + UNROLL - 1) // UNROLL
    return listed, rounds[None]


def dot_last(u, v):
    return lax.dot_general(u, v, (((1,), (1,)), ((), ())), preferred_element_type=F32)


def one_group(listed, rounds, w_ref, row, slabs, vectors, out_ref, prod, total, first):
    trials = prod.shape[1]
    width = prod.shape[2]
    slots = prod.shape[0]

    for n in range(slots):
        made = lax.dot_general(vectors(n), slabs(n), (((0,), (0,)), ((), ())), preferred_element_type=F32)
        prod[n] = made.astype(BF16)
    total[...] = jnp.zeros_like(total)

    def some(i, _):
        for d in range(0, UNROLL, 2):
            a, b = listed[i * UNROLL + d], listed[i * UNROLL + d + 1]
            both = jnp.concatenate([prod[a & 63], prod[b & 63]], axis=0)
            made = dot_last(both, w_ref[a >> 12, pl.ds(row, width), :])
            total[(a >> 6) & 63] += made[:trials]
            total[(b >> 6) & 63] += made[trials:]
        return 0

    lax.fori_loop(0, rounds[0], some, 0)
    for k in range(slots):
        made = dot_last(slabs(k), total[k].astype(BF16))

        if first:
            out_ref[k] = made
        else:
            out_ref[k] += made


def pack_kernel(core, source, *refs):
    outs, sems = refs[:-1], refs[-1]
    half_g, size = source.shape[2] // 2, outs[0].shape[2]
    if len(outs) == 1:
        starts = [pl.multiple_of((1 - core[0]) * half_g, size)]
    else:
        starts = [0, half_g]
    part = source.shape[0] // 4
    copies = [
        pltpu.make_async_copy(
            source.at[pl.ds(j * part, part), :, pl.ds(start, size)], out.at[pl.ds(j * part, part)], sems.at[i, j]
        )
        for i, (start, out) in enumerate(zip(starts, outs))
        for j in range(4)
    ]
    for copy in copies:
        copy.start()
    for copy in copies:
        copy.wait()


def density_kernel(core, own, vec, sib, vec_s, out):
    half_g = sib.shape[2]
    rows = lambda value: value.reshape(value.shape[0] * value.shape[1], value.shape[2])

    def over_pairs(v, d):
        return lax.dot_general(rows(v), rows(d), (((0,), (0,)), ((), ())), preferred_element_type=F32)

    mine = own[:, :, pl.ds(pl.multiple_of(core[0] * half_g, half_g), half_g)]
    out[...] = over_pairs(vec[...], mine) + over_pairs(vec_s[...], sib[...])


def near_kernel(start, count, load, *refs):
    if load:
        core, listed, rounds, own, vec, sib, vec_s, screen, out, w, prod, total, sems = refs
    else:
        core, listed, rounds, own, vec, sib, vec_s, w, _, out, prod, total = refs
    half, _, _ = own.shape
    width = prod.shape[2]
    half_g = w.shape[1]
    groups = half_g // width
    own_at = core[0] * half_g

    def copy(g):
        return pltpu.make_async_copy(
            screen.at[:, pl.ds(pl.multiple_of(own_at + g * width, width), width), :],
            w.at[:, pl.ds(g * width, width), :],
            sems.at[g],
        )

    if load:
        for g in range(groups):
            copy(g).start()
    for g in range(start, start + count):
        if load:
            copy(g).wait()
        at = pl.multiple_of(own_at + g * width, width)

        def slabs(n, at=at, g=g):
            return own[n, :, pl.ds(at, width)] if n < half else sib[n - half, :, g * width : (g + 1) * width]

        def vectors(n):
            return vec[n] if n < half else vec_s[n - half]

        one_group(listed, rounds, w, g * width, slabs, vectors, out, prod, total, load and g == start)
    if load:
        for g in range(start + count, groups):
            copy(g).wait()


def far_kernel(start, count, fresh, sources, core, listed, rounds, own, vec, sib, vec_s, w, vec_p, *refs):
    refs = refs[0 if fresh else 1 :]
    sources, (out, prod, total, came, sem) = refs[:sources], refs[sources:]
    half, _, _ = own.shape
    width = prod.shape[2]
    half_g = w.shape[1]
    own_at = core[0] * half_g
    if len(sources) == 1:
        pltpu.make_async_copy(sources[0], came, sem).start()
    else:

        @pl.when(core[0] == 0)
        def _():
            pltpu.make_async_copy(sources[0], came, sem).start()

        @pl.when(core[0] != 0)
        def _():
            pltpu.make_async_copy(sources[1], came, sem).start()

    pltpu.make_async_copy(sources[0], came, sem).wait()
    for g in range(start, start + count):
        at = pl.multiple_of(own_at + g * width, width)

        def slabs(n, at=at, g=g):
            if n >= half:
                return came[n - half, :, (g - start) * width : (g - start + 1) * width]
            return jnp.where(
                core[0] == 0, own[n, :, pl.ds(at, width)], sib[n, :, g * width : (g + 1) * width]
            )

        def vectors(n):
            if n >= half:
                return vec_p[n - half]
            return jnp.where(core[0] == 0, vec[n], vec_s[n])

        one_group(listed, rounds, w, g * width, slabs, vectors, out, prod, total, fresh and g == start)


def last_kernel(core, own, sib, s2, near, far, give, edge, inner):
    half, pairs, _ = own.shape
    trials, half_g = s2.shape
    width = 256
    own_at = core[0] * half_g

    def exchange(slab):
        acc = jnp.zeros((half * pairs, trials), F32)
        for g in range(half_g // width):
            acc += dot_last(slab(g).reshape(half * pairs, width), s2[:, g * width : (g + 1) * width])
        return acc.reshape(half, pairs, trials)

    mine = exchange(lambda g: own[:, :, pl.ds(pl.multiple_of(own_at + g * width, width), width)]) - near[:half]
    other = exchange(lambda g: sib[:, :, g * width : (g + 1) * width]) - near[half:]

    @pl.when(core[0] == 0)
    def _():
        edge[...] = mine - far[:half]
        inner[...] = other
        give[:half] = (-far[half:]).astype(BF16)
        give[half:] = other.astype(BF16)

    @pl.when(core[0] != 0)
    def _():
        edge[...] = -far[half:]
        inner[...] = mine
        give[:half] = (other - far[:half]).astype(BF16)
        give[half:] = mine.astype(BF16)


def density_steps(part, me, size):
    columns = part.shape[1] // 2
    high = (me // 2) % 2
    keep = lax.dynamic_slice_in_dim(part, high * columns, columns, 1)
    give = lax.dynamic_slice_in_dim(part, (1 - high) * columns, columns, 1).astype(BF16)
    part = keep + (yield give, 2).astype(F32)
    bit = 4
    while bit < size:
        part = part + (yield part.astype(BF16), bit).astype(F32)
        bit *= 2
    part = part.astype(BF16)
    other = yield part, 2
    return jnp.where(high == 0, jnp.concatenate([part, other], 1), jnp.concatenate([other, part], 1))


class Density:
    def __init__(self, steps, size):
        self.steps, self.size, self.result = steps, size, None
        self.send(None)

    def send(self, got):
        try:
            self.give, self.bit = self.steps.send(got)
        except StopIteration as stop:
            self.give, self.result = stop.value, stop.value

    def after(self, value):
        if self.result is None:
            came = lax.ppermute(self.give, "ka", [(i, i ^ self.bit) for i in range(self.size)])
            came, value = lax.optimization_barrier((came, value))
            self.send(came)
        return self.before(value)

    def before(self, value):
        self.give, value = lax.optimization_barrier((self.give, value))
        return value

    def finish(self):
        while self.result is None:
            self.after(jnp.zeros((1,), F32))
        return self.give


def on_device(pair_density, trial_vectors, energy, coulomb, screen, neighbors, live_count, q_index):
    local_k, pair_count, local_g = pair_density.shape
    trial_count = trial_vectors.shape[2]
    q_count, _, width = screen.shape
    slots = neighbors.shape[1]
    size, parts = lax.axis_size("ka"), lax.axis_size("ga")
    me, mine = lax.axis_index("ka"), lax.axis_index("ga")
    core = me % 2
    core_id = core.astype(jnp.int32)[None]
    half_g = local_g // 2
    groups = half_g // width
    sibling = [(i, i ^ 1) for i in range(size)]
    onward = [(i, (i + 2) % size) for i in range(size)]
    to_next = [[(i, (i + 1 + target) % size) for i in range(1, size, 2)] for target in range(2)]

    def pick(first, second):
        return jnp.where(core == 0, first, second)

    offset = (neighbors // local_k - me + 1) % size
    table = jnp.concatenate([offset * local_k + neighbors % local_k, q_index, live_count[:, None]], axis=1)
    table_s = lax.ppermute(table, "ka", sibling)
    vec_s = lax.ppermute(trial_vectors, "ka", sibling)
    edge = pick(table_s, table)
    table_p = lax.ppermute(edge, "ka", onward)

    def packed(core_id, last, count):
        return pl.pallas_call(
            pack_kernel,
            out_shape=[jax.ShapeDtypeStruct((local_k, pair_count, last), BF16)] * count,
            in_specs=[IN_SMEM, ANYWHERE],
            out_specs=[IN_VMEM] * count,
            scratch_shapes=[pltpu.SemaphoreType.DMA((count, 4))],
        )(core_id, pair_density)

    (give_half,) = packed(core_id, half_g, 1)
    first_pieces = packed(lax.optimization_barrier((core_id, edge))[0], width, 2)
    sib = lax.ppermute(give_half, "ka", sibling)
    own_half = lax.dynamic_slice_in_dim(pair_density, core * half_g, half_g, 2)
    came = [[lax.ppermute(piece, "ka", pairs) for piece, pairs in zip(first_pieces, to_next)]]

    def send_group(g, value):
        piece = pick(sib[:, :, g * width : (g + 1) * width], own_half[:, :, g * width : (g + 1) * width])
        piece, value = lax.optimization_barrier((piece, value))
        came.append([lax.ppermute(piece, "ka", onward)])
        piece, value = lax.optimization_barrier((piece, value))
        return value

    part = pl.pallas_call(
        density_kernel,
        out_shape=jax.ShapeDtypeStruct((trial_count, half_g), F32),
        in_specs=[IN_SMEM] + [IN_VMEM] * 4,
        out_specs=IN_VMEM,
        compiler_params=pltpu.CompilerParams(vmem_limit_bytes=12 << 20),
    )(core_id, pair_density, trial_vectors, sib, vec_s)
    density = Density(density_steps(part, me, size), size)
    my_coulomb = lax.dynamic_slice_in_dim(coulomb, core * half_g, half_g, 0)

    def columns(t):
        live = jnp.arange(slots, dtype=jnp.int32)[None, :] < t[:, 2 * slots :]
        near = t[:, :slots]
        return near // local_k, near % local_k, t[:, slots : 2 * slots], live

    row = jnp.broadcast_to(jnp.arange(local_k, dtype=jnp.int32)[:, None], (local_k, slots))
    flat = lambda u, v: jnp.concatenate([u.reshape(-1), v.reshape(-1)])
    length = 2 * local_k * slots + q_count
    length = (length + UNROLL - 1) // UNROLL * UNROLL

    def listing(u, v, u_slot, v_slot, u_valid, v_valid):
        return pair_list(
            flat(u_slot, v_slot),
            flat(row, row + local_k),
            flat(u[2], v[2]),
            flat(u[3] & u_valid, v[3] & v_valid),
            q_count,
            length,
            2 * local_k,
        )

    own_t, sib_t = columns(table), columns(table_s)
    own_cross, sib_cross = own_t[0] == 2 - 2 * core, sib_t[0] == 2 * core
    near_list, near_rounds = listing(
        own_t,
        sib_t,
        own_t[1] + local_k * own_cross,
        sib_t[1] + local_k * (sib_t[0] == 1),
        own_cross | (own_t[0] == 1),
        sib_cross | (sib_t[0] == 1),
    )

    sums = jax.ShapeDtypeStruct((2 * local_k, pair_count, trial_count), F32)
    work = [
        VMEM((2 * local_k, trial_count, width), BF16),
        VMEM((2 * local_k + 1, trial_count, width), F32),
    ]

    def params():
        return pltpu.CompilerParams(vmem_limit_bytes=12 << 20)

    def cost(count, pairs):
        return pl.CostEstimate(
            flops=4 * count * pairs * width * width * trial_count, transcendentals=0, bytes_accessed=1 << 20
        )

    a_t, p_t = columns(pick(table, table_s)), columns(table_p)
    far_list, far_rounds = listing(a_t, p_t, a_t[1] + local_k, p_t[1], a_t[0] == 0, p_t[0] == 2)
    near_rounds, far_list, far_rounds = lax.optimization_barrier((near_rounds, far_list, far_rounds))
    near_rounds = density.before(near_rounds)
    near, w_half = pl.pallas_call(
        functools.partial(near_kernel, 0, 1, True),
        out_shape=(sums, jax.ShapeDtypeStruct((q_count, half_g, width), BF16)),
        in_specs=[IN_SMEM] * 3 + [IN_VMEM] * 4 + [ANYWHERE],
        out_specs=(IN_VMEM, IN_VMEM),
        scratch_shapes=work + [pltpu.SemaphoreType.DMA((groups,))],
        compiler_params=params(),
        cost_estimate=cost(1, 160),
    )(core_id, near_list, near_rounds, pair_density, trial_vectors, sib, vec_s, screen)
    near = density.after(near)
    edge_vec, near = lax.optimization_barrier((pick(vec_s, trial_vectors), near))
    vec_p = lax.ppermute(edge_vec, "ka", onward)
    for start, count, going in ((1, 1, (1,)), (2, groups - 2, range(2, groups))):
        if count < 1 or start >= groups:
            continue
        if start == 2:
            near, vec_p, *came[0] = lax.optimization_barrier((near, vec_p, *came[0]))
        for g in going:
            near = send_group(g, near)
        near = pl.pallas_call(
            functools.partial(near_kernel, start, count, False),
            out_shape=sums,
            in_specs=[IN_SMEM] * 3 + [IN_VMEM] * 6,
            out_specs=IN_VMEM,
            scratch_shapes=work,
            input_output_aliases={8: 0},
            compiler_params=params(),
            cost_estimate=cost(count, 160),
        )(core_id, near_list, near_rounds, pair_density, trial_vectors, sib, vec_s, w_half, near)
        if start == 1:
            near = density.after(near)
    near, far_rounds = lax.optimization_barrier((near, far_rounds))
    far = None
    for c in range(groups):
        far = pl.pallas_call(
            functools.partial(far_kernel, c, 1, c == 0, len(came[c])),
            out_shape=sums,
            in_specs=[IN_SMEM] * 3 + [IN_VMEM] * (6 + (c > 0)) + [ANYWHERE] * len(came[c]),
            out_specs=IN_VMEM,
            scratch_shapes=work
            + [VMEM((local_k, pair_count, width), BF16), pltpu.SemaphoreType.DMA],
            input_output_aliases={9: 0} if c else {},
            compiler_params=params(),
            cost_estimate=cost(1, 8),
        )(
            core_id, far_list, far_rounds, pair_density, trial_vectors, sib, vec_s, w_half, vec_p,
            *([far] if c else []), *came[c],
        )
        if c >= groups - 2:
            far = density.after(far)
    screened2 = (2.0 * my_coulomb[None, :] * density.finish().astype(F32)).astype(BF16)
    half_sums = jax.ShapeDtypeStruct((local_k, pair_count, trial_count), F32)
    give, edge, inner = pl.pallas_call(
        last_kernel,
        out_shape=(jax.ShapeDtypeStruct(sums.shape, BF16), half_sums, half_sums),
        in_specs=[IN_SMEM] + [IN_VMEM] * 5,
        out_specs=(IN_VMEM,) * 3,
        compiler_params=params(),
        cost_estimate=cost(1, 16),
    )(core_id, pair_density, sib, screened2, near, far)

    got = lax.ppermute(give, "ka", sibling)
    edge, inner = edge + got[:local_k].astype(F32), inner + got[local_k:].astype(F32)
    rows = pair_count // parts
    rows_of = lambda value, at: lax.dynamic_slice_in_dim(value, at * rows, rows, 1)
    stay = lambda first: [(i, i) for i in range(first, size, 2)]
    back = [(i, (i - 2) % size) for i in range(1, size, 2)]

    def sent(value, steps, ka_pairs):
        pairs = [
            (s * parts + g, d * parts + (g + steps) % parts) for s, d in ka_pairs for g in range(parts)
        ]
        return lax.ppermute(
            rows_of(value, (mine + steps) % parts).astype(BF16), ("ka", "ga"), pairs
        ).astype(F32)

    answer = jnp.where(core == 0, rows_of(edge, mine), rows_of(inner, mine))
    answer = answer + sent(edge, 0, back)
    for steps in range(1, parts):
        answer = answer + sent(edge, steps, stay(0) + back) + sent(inner, steps, stay(1))
    energy_rows = lax.dynamic_slice_in_dim(energy, mine * rows, rows, 1)
    vector_rows = lax.dynamic_slice_in_dim(trial_vectors, mine * rows, rows, 1)
    return (energy_rows[:, :, None] * vector_rows.astype(F32) + answer).astype(BF16)


def solution(mesh):
    in_specs = (
        P("ka", None, "ga"),
        P("ka", None, None),
        P("ka", None),
        P("ga"),
        P(None, "ga", None),
        P("ka", None),
        P("ka"),
        P("ka", None),
    )
    out_specs = P("ka", "ga", None)
    return jax.shard_map(
        on_device, mesh=mesh, in_specs=in_specs, out_specs=out_specs, check_vma=False
    )
```

```python
import functools

import jax
import jax.numpy as jnp
from jax import lax
from jax.experimental import pallas as pl
from jax.experimental.pallas import tpu as pltpu
from jax.sharding import PartitionSpec as P

UNROLL = 32
F32, BF16 = jnp.float32, jnp.bfloat16
VMEM, SMEM = pltpu.VMEM, pltpu.SMEM
IN_VMEM, IN_SMEM, ANYWHERE = (pl.BlockSpec(memory_space=space) for space in (VMEM, SMEM, pl.ANY))


def pair_list(n_slot, k_slot, q, valid, q_count, length, spare):
    entries = q.shape[0]
    order = jnp.arange(entries, dtype=jnp.int32)
    qs = jnp.arange(q_count, dtype=jnp.int32)
    same = (q[:, None] == q[None, :]) & valid[None, :] & (order[None, :] < order[:, None])
    within = jnp.sum(same.astype(jnp.int32), axis=1)
    count = jnp.sum(((q[None, :] == qs[:, None]) & valid[None, :]).astype(jnp.int32), axis=1)
    padded = (count + 1) // 2 * 2
    base = jnp.sum(jnp.where(qs[None, :] < q[:, None], padded[None, :], 0), axis=1)
    place = jnp.where(valid, base + within, -1)
    code = n_slot + 64 * k_slot + 4096 * q
    blank = 64 * spare
    rows = jnp.arange(length, dtype=jnp.int32)
    listed = blank + jnp.sum(jnp.where(place[None, :] == rows[:, None], code[None, :] - blank, 0), axis=1)
    rounds = (jnp.sum(padded) + UNROLL - 1) // UNROLL
    return listed, rounds[None]


def dot_last(u, v):
    return lax.dot_general(u, v, (((1,), (1,)), ((), ())), preferred_element_type=F32)


def one_group(listed, rounds, w_ref, row, slabs, vectors, out_ref, prod, total, first):
    trials = prod.shape[1]
    width = prod.shape[2]
    slots = prod.shape[0]

    for n in range(slots):
        made = lax.dot_general(vectors(n), slabs(n), (((0,), (0,)), ((), ())), preferred_element_type=F32)
        prod[n] = made.astype(BF16)
    total[...] = jnp.zeros_like(total)

    def some(i, _):
        for d in range(0, UNROLL, 2):
            a, b = listed[i * UNROLL + d], listed[i * UNROLL + d + 1]
            both = jnp.concatenate([prod[a & 63], prod[b & 63]], axis=0)
            made = dot_last(both, w_ref[a >> 12, pl.ds(row, width), :])
            total[(a >> 6) & 63] += made[:trials]
            total[(b >> 6) & 63] += made[trials:]
        return 0

    lax.fori_loop(0, rounds[0], some, 0)
    for k in range(slots):
        made = dot_last(slabs(k), total[k].astype(BF16))

        if first:
            out_ref[k] = made
        else:
            out_ref[k] += made


def pack_kernel(core, source, *refs):
    outs, sems = refs[:-1], refs[-1]
    half_g, size = source.shape[2] // 2, outs[0].shape[2]
    if len(outs) == 1:
        starts = [pl.multiple_of((1 - core[0]) * half_g, size)]
    else:
        starts = [0, half_g]
    part = source.shape[0] // 4
    copies = [
        pltpu.make_async_copy(
            source.at[pl.ds(j * part, part), :, pl.ds(start, size)], out.at[pl.ds(j * part, part)], sems.at[i, j]
        )
        for i, (start, out) in enumerate(zip(starts, outs))
        for j in range(4)
    ]
    for copy in copies:
        copy.start()
    for copy in copies:
        copy.wait()


def density_kernel(core, own, vec, sib, vec_s, out):
    half_g = sib.shape[2]
    rows = lambda value: value.reshape(value.shape[0] * value.shape[1], value.shape[2])

    def over_pairs(v, d):
        return lax.dot_general(rows(v), rows(d), (((0,), (0,)), ((), ())), preferred_element_type=F32)

    mine = own[:, :, pl.ds(pl.multiple_of(core[0] * half_g, half_g), half_g)]
    out[...] = over_pairs(vec[...], mine) + over_pairs(vec_s[...], sib[...])


def near_kernel(start, count, load, *refs):
    if load:
        core, listed, rounds, own, vec, sib, vec_s, screen, out, w, prod, total, sems = refs
    else:
        core, listed, rounds, own, vec, sib, vec_s, w, _, out, prod, total = refs
    half, _, _ = own.shape
    width = prod.shape[2]
    half_g = w.shape[1]
    groups = half_g // width
    own_at = core[0] * half_g

    def copy(g):
        return pltpu.make_async_copy(
            screen.at[:, pl.ds(pl.multiple_of(own_at + g * width, width), width), :],
            w.at[:, pl.ds(g * width, width), :],
            sems.at[g],
        )

    if load:
        for g in range(groups):
            copy(g).start()
    for g in range(start, start + count):
        if load:
            copy(g).wait()
        at = pl.multiple_of(own_at + g * width, width)

        def slabs(n, at=at, g=g):
            return own[n, :, pl.ds(at, width)] if n < half else sib[n - half, :, g * width : (g + 1) * width]

        def vectors(n):
            return vec[n] if n < half else vec_s[n - half]

        one_group(listed, rounds, w, g * width, slabs, vectors, out, prod, total, load and g == start)
    if load:
        for g in range(start + count, groups):
            copy(g).wait()


def far_kernel(start, count, fresh, sources, core, listed, rounds, own, vec, sib, vec_s, w, vec_p, *refs):
    refs = refs[0 if fresh else 1 :]
    sources, (out, prod, total, came, sem) = refs[:sources], refs[sources:]
    half, _, _ = own.shape
    width = prod.shape[2]
    half_g = w.shape[1]
    own_at = core[0] * half_g
    if len(sources) == 1:
        pltpu.make_async_copy(sources[0], came, sem).start()
    else:

        @pl.when(core[0] == 0)
        def _():
            pltpu.make_async_copy(sources[0], came, sem).start()

        @pl.when(core[0] != 0)
        def _():
            pltpu.make_async_copy(sources[1], came, sem).start()

    pltpu.make_async_copy(sources[0], came, sem).wait()
    for g in range(start, start + count):
        at = pl.multiple_of(own_at + g * width, width)

        def slabs(n, at=at, g=g):
            if n >= half:
                return came[n - half, :, (g - start) * width : (g - start + 1) * width]
            return jnp.where(
                core[0] == 0, own[n, :, pl.ds(at, width)], sib[n, :, g * width : (g + 1) * width]
            )

        def vectors(n):
            if n >= half:
                return vec_p[n - half]
            return jnp.where(core[0] == 0, vec[n], vec_s[n])

        one_group(listed, rounds, w, g * width, slabs, vectors, out, prod, total, fresh and g == start)


def last_kernel(core, own, sib, s2, near, far, give, edge, inner):
    half, pairs, _ = own.shape
    trials, half_g = s2.shape
    width = 256
    own_at = core[0] * half_g

    def exchange(slab):
        acc = jnp.zeros((half * pairs, trials), F32)
        for g in range(half_g // width):
            acc += dot_last(slab(g).reshape(half * pairs, width), s2[:, g * width : (g + 1) * width])
        return acc.reshape(half, pairs, trials)

    mine = exchange(lambda g: own[:, :, pl.ds(pl.multiple_of(own_at + g * width, width), width)]) - near[:half]
    other = exchange(lambda g: sib[:, :, g * width : (g + 1) * width]) - near[half:]

    @pl.when(core[0] == 0)
    def _():
        edge[...] = mine - far[:half]
        inner[...] = other
        give[:half] = (-far[half:]).astype(BF16)
        give[half:] = other.astype(BF16)

    @pl.when(core[0] != 0)
    def _():
        edge[...] = -far[half:]
        inner[...] = mine
        give[:half] = (other - far[:half]).astype(BF16)
        give[half:] = mine.astype(BF16)


def density_steps(part, me, size):
    low = [i for i in range(size) if (i // 2) % 2 == 0]
    part = part + (yield part.astype(BF16), [(i ^ 2, i) for i in low]).astype(F32)
    bit = 4
    while bit < size:
        part = part + (yield part.astype(BF16), [(i, i ^ bit) for i in low]).astype(F32)
        bit *= 2
    part = part.astype(BF16)
    other = yield part, [(i, i ^ 2) for i in low]
    return jnp.where((me // 2) % 2 == 0, part, other)


class Density:
    def __init__(self, steps):
        self.steps, self.result = steps, None
        self.send(None)

    def send(self, got):
        try:
            self.give, self.pairs = self.steps.send(got)
        except StopIteration as stop:
            self.give, self.result = stop.value, stop.value

    def after(self, value):
        if self.result is None:
            came = lax.ppermute(self.give, "ka", self.pairs)
            came, value = lax.optimization_barrier((came, value))
            self.send(came)
        return self.before(value)

    def before(self, value):
        self.give, value = lax.optimization_barrier((self.give, value))
        return value

    def finish(self):
        while self.result is None:
            self.after(jnp.zeros((1,), F32))
        return self.give


def on_device(pair_density, trial_vectors, energy, coulomb, screen, neighbors, live_count, q_index):
    local_k, pair_count, local_g = pair_density.shape
    trial_count = trial_vectors.shape[2]
    q_count, _, width = screen.shape
    slots = neighbors.shape[1]
    size, parts = lax.axis_size("ka"), lax.axis_size("ga")
    me, mine = lax.axis_index("ka"), lax.axis_index("ga")
    core = me % 2
    core_id = core.astype(jnp.int32)[None]
    half_g = local_g // 2
    groups = half_g // width
    sibling = [(i, i ^ 1) for i in range(size)]
    onward = [(i, (i + 2) % size) for i in range(size)]
    to_next = [[(i, (i + 1 + target) % size) for i in range(1, size, 2)] for target in range(2)]

    def pick(first, second):
        return jnp.where(core == 0, first, second)

    offset = (neighbors // local_k - me + 1) % size
    table = jnp.concatenate([offset * local_k + neighbors % local_k, q_index, live_count[:, None]], axis=1)
    table_s = lax.ppermute(table, "ka", sibling)
    vec_s = lax.ppermute(trial_vectors, "ka", sibling)
    edge = pick(table_s, table)
    table_p = lax.ppermute(edge, "ka", onward)

    def packed(core_id, last, count):
        return pl.pallas_call(
            pack_kernel,
            out_shape=[jax.ShapeDtypeStruct((local_k, pair_count, last), BF16)] * count,
            in_specs=[IN_SMEM, ANYWHERE],
            out_specs=[IN_VMEM] * count,
            scratch_shapes=[pltpu.SemaphoreType.DMA((count, 4))],
        )(core_id, pair_density)

    (give_half,) = packed(core_id, half_g, 1)
    first_pieces = packed(lax.optimization_barrier((core_id, edge))[0], width, 2)
    sib = lax.ppermute(give_half, "ka", sibling)
    own_half = lax.dynamic_slice_in_dim(pair_density, core * half_g, half_g, 2)
    came = [[lax.ppermute(piece, "ka", pairs) for piece, pairs in zip(first_pieces, to_next)]]

    def send_group(g, value):
        piece = pick(sib[:, :, g * width : (g + 1) * width], own_half[:, :, g * width : (g + 1) * width])
        piece, value = lax.optimization_barrier((piece, value))
        came.append([lax.ppermute(piece, "ka", onward)])
        piece, value = lax.optimization_barrier((piece, value))
        return value

    part = pl.pallas_call(
        density_kernel,
        out_shape=jax.ShapeDtypeStruct((trial_count, half_g), F32),
        in_specs=[IN_SMEM] + [IN_VMEM] * 4,
        out_specs=IN_VMEM,
        compiler_params=pltpu.CompilerParams(vmem_limit_bytes=12 << 20),
    )(core_id, pair_density, trial_vectors, sib, vec_s)
    density = Density(density_steps(part, me, size))
    my_coulomb = lax.dynamic_slice_in_dim(coulomb, core * half_g, half_g, 0)

    def columns(t):
        live = jnp.arange(slots, dtype=jnp.int32)[None, :] < t[:, 2 * slots :]
        near = t[:, :slots]
        return near // local_k, near % local_k, t[:, slots : 2 * slots], live

    row = jnp.broadcast_to(jnp.arange(local_k, dtype=jnp.int32)[:, None], (local_k, slots))
    flat = lambda u, v: jnp.concatenate([u.reshape(-1), v.reshape(-1)])
    length = 2 * local_k * slots + q_count
    length = (length + UNROLL - 1) // UNROLL * UNROLL

    def listing(u, v, u_slot, v_slot, u_valid, v_valid):
        return pair_list(
            flat(u_slot, v_slot),
            flat(row, row + local_k),
            flat(u[2], v[2]),
            flat(u[3] & u_valid, v[3] & v_valid),
            q_count,
            length,
            2 * local_k,
        )

    own_t, sib_t = columns(table), columns(table_s)
    own_cross, sib_cross = own_t[0] == 2 - 2 * core, sib_t[0] == 2 * core
    near_list, near_rounds = listing(
        own_t,
        sib_t,
        own_t[1] + local_k * own_cross,
        sib_t[1] + local_k * (sib_t[0] == 1),
        own_cross | (own_t[0] == 1),
        sib_cross | (sib_t[0] == 1),
    )

    sums = jax.ShapeDtypeStruct((2 * local_k, pair_count, trial_count), F32)
    work = [
        VMEM((2 * local_k, trial_count, width), BF16),
        VMEM((2 * local_k + 1, trial_count, width), F32),
    ]

    def params():
        return pltpu.CompilerParams(vmem_limit_bytes=12 << 20)

    def cost(count, pairs):
        return pl.CostEstimate(
            flops=4 * count * pairs * width * width * trial_count, transcendentals=0, bytes_accessed=1 << 20
        )

    a_t, p_t = columns(pick(table, table_s)), columns(table_p)
    far_list, far_rounds = listing(a_t, p_t, a_t[1] + local_k, p_t[1], a_t[0] == 0, p_t[0] == 2)
    near_rounds, far_list, far_rounds = lax.optimization_barrier((near_rounds, far_list, far_rounds))
    near_rounds = density.before(near_rounds)
    if groups > 1:
        near_rounds = send_group(1, near_rounds)
    near, w_half = pl.pallas_call(
        functools.partial(near_kernel, 0, 1, True),
        out_shape=(sums, jax.ShapeDtypeStruct((q_count, half_g, width), BF16)),
        in_specs=[IN_SMEM] * 3 + [IN_VMEM] * 4 + [ANYWHERE],
        out_specs=(IN_VMEM, IN_VMEM),
        scratch_shapes=work + [pltpu.SemaphoreType.DMA((groups,))],
        compiler_params=params(),
        cost_estimate=cost(1, 160),
    )(core_id, near_list, near_rounds, pair_density, trial_vectors, sib, vec_s, screen)
    edge_vec, near = lax.optimization_barrier((pick(vec_s, trial_vectors), near))
    vec_p = lax.ppermute(edge_vec, "ka", onward)
    near, *came[0] = lax.optimization_barrier((near, *came[0]))
    for start, count, going in ((1, 1, range(2, min(groups, 3))), (2, groups - 2, range(3, groups))):
        if count < 1 or start >= groups:
            continue
        for g in going:
            near = send_group(g, near)
        near = pl.pallas_call(
            functools.partial(near_kernel, start, count, False),
            out_shape=sums,
            in_specs=[IN_SMEM] * 3 + [IN_VMEM] * 6,
            out_specs=IN_VMEM,
            scratch_shapes=work,
            input_output_aliases={8: 0},
            compiler_params=params(),
            cost_estimate=cost(count, 160),
        )(core_id, near_list, near_rounds, pair_density, trial_vectors, sib, vec_s, w_half, near)
        near = density.after(near)
    near, far_rounds = lax.optimization_barrier((near, far_rounds))
    far = None
    for c in range(groups):
        far = pl.pallas_call(
            functools.partial(far_kernel, c, 1, c == 0, len(came[c])),
            out_shape=sums,
            in_specs=[IN_SMEM] * 3 + [IN_VMEM] * (6 + (c > 0)) + [ANYWHERE] * len(came[c]),
            out_specs=IN_VMEM,
            scratch_shapes=work
            + [VMEM((local_k, pair_count, width), BF16), pltpu.SemaphoreType.DMA],
            input_output_aliases={9: 0} if c else {},
            compiler_params=params(),
            cost_estimate=cost(1, 80),
        )(
            core_id, far_list, far_rounds, pair_density, trial_vectors, sib, vec_s, w_half, vec_p,
            *([far] if c else []), *came[c],
        )
        if c in (groups - 3, groups - 1):
            far = density.after(far)
    screened2 = (2.0 * my_coulomb[None, :] * density.finish().astype(F32)).astype(BF16)
    half_sums = jax.ShapeDtypeStruct((local_k, pair_count, trial_count), F32)
    give, edge, inner = pl.pallas_call(
        last_kernel,
        out_shape=(jax.ShapeDtypeStruct(sums.shape, BF16), half_sums, half_sums),
        in_specs=[IN_SMEM] + [IN_VMEM] * 5,
        out_specs=(IN_VMEM,) * 3,
        compiler_params=params(),
        cost_estimate=cost(1, 16),
    )(core_id, pair_density, sib, screened2, near, far)

    got = lax.ppermute(give, "ka", sibling)
    edge, inner = edge + got[:local_k].astype(F32), inner + got[local_k:].astype(F32)
    rows = pair_count // parts
    rows_of = lambda value, at: lax.dynamic_slice_in_dim(value, at * rows, rows, 1)
    stay = lambda first: [(i, i) for i in range(first, size, 2)]
    back = [(i, (i - 2) % size) for i in range(1, size, 2)]

    def sent(value, steps, ka_pairs):
        pairs = [
            (s * parts + g, d * parts + (g + steps) % parts) for s, d in ka_pairs for g in range(parts)
        ]
        return lax.ppermute(
            rows_of(value, (mine + steps) % parts).astype(BF16), ("ka", "ga"), pairs
        ).astype(F32)

    answer = jnp.where(core == 0, rows_of(edge, mine), rows_of(inner, mine))
    answer = answer + sent(edge, 0, back)
    for steps in range(1, parts):
        answer = answer + sent(edge, steps, stay(0) + back) + sent(inner, steps, stay(1))
    energy_rows = lax.dynamic_slice_in_dim(energy, mine * rows, rows, 1)
    vector_rows = lax.dynamic_slice_in_dim(trial_vectors, mine * rows, rows, 1)
    return (energy_rows[:, :, None] * vector_rows.astype(F32) + answer).astype(BF16)


def solution(mesh):
    in_specs = (
        P("ka", None, "ga"),
        P("ka", None, None),
        P("ka", None),
        P("ga"),
        P(None, "ga", None),
        P("ka", None),
        P("ka"),
        P("ka", None),
    )
    out_specs = P("ka", "ga", None)
    return jax.shard_map(
        on_device, mesh=mesh, in_specs=in_specs, out_specs=out_specs, check_vma=False
    )
```

```python
import functools

import jax
import jax.numpy as jnp
from jax import lax
from jax.experimental import pallas as pl
from jax.experimental.pallas import tpu as pltpu
from jax.sharding import PartitionSpec as P

UNROLL = 32
F32, BF16 = jnp.float32, jnp.bfloat16
VMEM, SMEM = pltpu.VMEM, pltpu.SMEM
IN_VMEM, IN_SMEM, ANYWHERE = (pl.BlockSpec(memory_space=space) for space in (VMEM, SMEM, pl.ANY))


def pair_list(n_slot, k_slot, q, valid, q_count, length, spare):
    entries = q.shape[0]
    order = jnp.arange(entries, dtype=jnp.int32)
    qs = jnp.arange(q_count, dtype=jnp.int32)
    same = (q[:, None] == q[None, :]) & valid[None, :] & (order[None, :] < order[:, None])
    within = jnp.sum(same.astype(jnp.int32), axis=1)
    count = jnp.sum(((q[None, :] == qs[:, None]) & valid[None, :]).astype(jnp.int32), axis=1)
    padded = (count + 1) // 2 * 2
    base = jnp.sum(jnp.where(qs[None, :] < q[:, None], padded[None, :], 0), axis=1)
    place = jnp.where(valid, base + within, -1)
    code = n_slot + 64 * k_slot + 4096 * q
    blank = 64 * spare
    rows = jnp.arange(length, dtype=jnp.int32)
    listed = blank + jnp.sum(jnp.where(place[None, :] == rows[:, None], code[None, :] - blank, 0), axis=1)
    pairs = jnp.sum(padded)
    left = pairs % UNROLL
    rounds = jnp.stack([(pairs + UNROLL // 2 - 1) // UNROLL, ((left > 0) & (left <= UNROLL // 2)).astype(jnp.int32)])
    return listed, rounds


def dot_last(u, v):
    return lax.dot_general(u, v, (((1,), (1,)), ((), ())), preferred_element_type=F32)


def one_group(listed, rounds, w_ref, row, slabs, vectors, out_ref, prod, total, first):
    trials = prod.shape[1]
    width = prod.shape[2]
    slots = prod.shape[0]

    for n in range(slots):
        made = lax.dot_general(vectors(n), slabs(n), (((0,), (0,)), ((), ())), preferred_element_type=F32)
        prod[n] = made.astype(BF16)
    total[...] = jnp.zeros_like(total)

    def some(start, count):
        for d in range(0, count, 2):
            a, b = listed[start + d], listed[start + d + 1]
            both = jnp.concatenate([prod[a & 63], prod[b & 63]], axis=0)
            made = dot_last(both, w_ref[a >> 12, pl.ds(row, width), :])
            total[(a >> 6) & 63] += made[:trials]
            total[(b >> 6) & 63] += made[trials:]

    def whole_round(i, _):
        some(i * UNROLL, UNROLL)
        return 0

    lax.fori_loop(0, rounds[0], whole_round, 0)

    @pl.when(rounds[1] > 0)
    def _():
        some(rounds[0] * UNROLL, UNROLL // 2)

    for k in range(slots):
        made = dot_last(slabs(k), total[k].astype(BF16))

        if first:
            out_ref[k] = made
        else:
            out_ref[k] += made


def pack_kernel(core, source, give, first, second, sems):
    half_g, width = give.shape[2], first.shape[2]
    part = source.shape[0] // 4
    away = pl.multiple_of((1 - core[0]) * half_g, half_g)
    copies = [
        pltpu.make_async_copy(
            source.at[pl.ds(j * part, part), :, pl.ds(start, out.shape[2])], out.at[pl.ds(j * part, part)], sems.at[i, j]
        )
        for i, (start, out) in enumerate(((away, give), (0, first), (half_g, second)))
        for j in range(4)
    ]
    for copy in copies:
        copy.start()
    for copy in copies:
        copy.wait()


def density_kernel(core, own, vec, sib, vec_s, out):
    half_g = sib.shape[2]
    rows = lambda value: value.reshape(value.shape[0] * value.shape[1], value.shape[2])

    def over_pairs(v, d):
        return lax.dot_general(rows(v), rows(d), (((0,), (0,)), ((), ())), preferred_element_type=F32)

    mine = own[:, :, pl.ds(pl.multiple_of(core[0] * half_g, half_g), half_g)]
    out[...] = over_pairs(vec[...], mine) + over_pairs(vec_s[...], sib[...])


def near_kernel(start, count, load, *refs):
    if load:
        core, listed, rounds, own, vec, sib, vec_s, screen, out, w, prod, total, sems = refs
    else:
        core, listed, rounds, own, vec, sib, vec_s, w, _, out, prod, total = refs
    half, _, _ = own.shape
    width = prod.shape[2]
    half_g = w.shape[1]
    groups = half_g // width
    own_at = core[0] * half_g

    def copy(g):
        return pltpu.make_async_copy(
            screen.at[:, pl.ds(pl.multiple_of(own_at + g * width, width), width), :],
            w.at[:, pl.ds(g * width, width), :],
            sems.at[g],
        )

    if load:
        for g in range(groups):
            copy(g).start()
    for g in range(start, start + count):
        if load:
            copy(g).wait()
        at = pl.multiple_of(own_at + g * width, width)

        def slabs(n, at=at, g=g):
            return own[n, :, pl.ds(at, width)] if n < half else sib[n - half, :, g * width : (g + 1) * width]

        def vectors(n):
            return vec[n] if n < half else vec_s[n - half]

        one_group(listed, rounds, w, g * width, slabs, vectors, out, prod, total, load and g == start)
    if load:
        for g in range(start + count, groups):
            copy(g).wait()


def far_kernel(start, count, fresh, sources, core, listed, rounds, own, vec, sib, vec_s, w, vec_p, *refs):
    refs = refs[0 if fresh else 1 :]
    sources, (out, prod, total, came, sem) = refs[:sources], refs[sources:]
    half, _, _ = own.shape
    width = prod.shape[2]
    half_g = w.shape[1]
    own_at = core[0] * half_g
    if len(sources) == 1:
        pltpu.make_async_copy(sources[0], came, sem).start()
    else:

        @pl.when(core[0] == 0)
        def _():
            pltpu.make_async_copy(sources[0], came, sem).start()

        @pl.when(core[0] != 0)
        def _():
            pltpu.make_async_copy(sources[1], came, sem).start()

    pltpu.make_async_copy(sources[0], came, sem).wait()
    for g in range(start, start + count):
        at = pl.multiple_of(own_at + g * width, width)

        def slabs(n, at=at, g=g):
            if n >= half:
                return came[n - half, :, (g - start) * width : (g - start + 1) * width]
            return jnp.where(
                core[0] == 0, own[n, :, pl.ds(at, width)], sib[n, :, g * width : (g + 1) * width]
            )

        def vectors(n):
            if n >= half:
                return vec_p[n - half]
            return jnp.where(core[0] == 0, vec[n], vec_s[n])

        one_group(listed, rounds, w, g * width, slabs, vectors, out, prod, total, fresh and g == start)


def last_kernel(core, own, sib, s2, near, far, give, edge, inner):
    half, pairs, _ = own.shape
    trials, half_g = s2.shape
    width = 256
    own_at = core[0] * half_g

    def exchange(slab):
        acc = jnp.zeros((half * pairs, trials), F32)
        for g in range(half_g // width):
            acc += dot_last(slab(g).reshape(half * pairs, width), s2[:, g * width : (g + 1) * width])
        return acc.reshape(half, pairs, trials)

    mine = exchange(lambda g: own[:, :, pl.ds(pl.multiple_of(own_at + g * width, width), width)]) - near[:half]
    other = exchange(lambda g: sib[:, :, g * width : (g + 1) * width]) - near[half:]

    @pl.when(core[0] == 0)
    def _():
        edge[...] = mine - far[:half]
        inner[...] = other
        give[:half] = (-far[half:]).astype(BF16)
        give[half:] = other.astype(BF16)

    @pl.when(core[0] != 0)
    def _():
        edge[...] = -far[half:]
        inner[...] = mine
        give[:half] = (other - far[:half]).astype(BF16)
        give[half:] = mine.astype(BF16)


def density_steps(part, me, size):
    low = [i for i in range(size) if (i // 2) % 2 == 0]
    part = part + (yield part.astype(BF16), [(i ^ 2, i) for i in low]).astype(F32)
    bit = 4
    while bit < size:
        part = part + (yield part.astype(BF16), [(i, i ^ bit) for i in low]).astype(F32)
        bit *= 2
    part = part.astype(BF16)
    other = yield part, [(i, i ^ 2) for i in low]
    return jnp.where((me // 2) % 2 == 0, part, other)


class Density:
    def __init__(self, steps):
        self.steps, self.result = steps, None
        self.send(None)

    def send(self, got):
        try:
            self.give, self.pairs = self.steps.send(got)
        except StopIteration as stop:
            self.give, self.result = stop.value, stop.value

    def after(self, value):
        if self.result is None:
            came = lax.ppermute(self.give, "ka", self.pairs)
            came, value = lax.optimization_barrier((came, value))
            self.send(came)
        return self.before(value)

    def before(self, value):
        self.give, value = lax.optimization_barrier((self.give, value))
        return value

    def finish(self):
        while self.result is None:
            self.after(jnp.zeros((1,), F32))
        return self.give


def on_device(pair_density, trial_vectors, energy, coulomb, screen, neighbors, live_count, q_index):
    local_k, pair_count, local_g = pair_density.shape
    trial_count = trial_vectors.shape[2]
    q_count, _, width = screen.shape
    slots = neighbors.shape[1]
    size, parts = lax.axis_size("ka"), lax.axis_size("ga")
    me, mine = lax.axis_index("ka"), lax.axis_index("ga")
    core = me % 2
    core_id = core.astype(jnp.int32)[None]
    half_g = local_g // 2
    groups = half_g // width
    sibling = [(i, i ^ 1) for i in range(size)]
    onward = [(i, (i + 2) % size) for i in range(size)]
    to_next = [[(i, (i + 1 + target) % size) for i in range(1, size, 2)] for target in range(2)]

    def pick(first, second):
        return jnp.where(core == 0, first, second)

    offset = (neighbors // local_k - me + 1) % size
    table = jnp.concatenate([offset * local_k + neighbors % local_k, q_index, live_count[:, None]], axis=1)
    table_s = lax.ppermute(table, "ka", sibling)
    vec_s = lax.ppermute(trial_vectors, "ka", sibling)
    edge = pick(table_s, table)
    table_p = lax.ppermute(edge, "ka", onward)

    sent = lambda last: jax.ShapeDtypeStruct((local_k, pair_count, last), BF16)
    give_half, *first_pieces = pl.pallas_call(
        pack_kernel,
        out_shape=(sent(half_g), sent(width), sent(width)),
        in_specs=[IN_SMEM, ANYWHERE],
        out_specs=(IN_VMEM,) * 3,
        scratch_shapes=[pltpu.SemaphoreType.DMA((3, 4))],
    )(core_id, pair_density)
    *first_pieces, _ = lax.optimization_barrier((*first_pieces, edge))
    sib = lax.ppermute(give_half, "ka", sibling)
    own_half = lax.dynamic_slice_in_dim(pair_density, core * half_g, half_g, 2)
    came = [[lax.ppermute(piece, "ka", pairs) for piece, pairs in zip(first_pieces, to_next)]]

    def send_group(g, value):
        piece = pick(sib[:, :, g * width : (g + 1) * width], own_half[:, :, g * width : (g + 1) * width])
        piece, value = lax.optimization_barrier((piece, value))
        came.append([lax.ppermute(piece, "ka", onward)])
        piece, value = lax.optimization_barrier((piece, value))
        return value

    part = pl.pallas_call(
        density_kernel,
        out_shape=jax.ShapeDtypeStruct((trial_count, half_g), F32),
        in_specs=[IN_SMEM] + [IN_VMEM] * 4,
        out_specs=IN_VMEM,
        compiler_params=pltpu.CompilerParams(vmem_limit_bytes=12 << 20),
    )(core_id, pair_density, trial_vectors, sib, vec_s)
    density = Density(density_steps(part, me, size))
    my_coulomb = lax.dynamic_slice_in_dim(coulomb, core * half_g, half_g, 0)

    def columns(t):
        live = jnp.arange(slots, dtype=jnp.int32)[None, :] < t[:, 2 * slots :]
        near = t[:, :slots]
        return near // local_k, near % local_k, t[:, slots : 2 * slots], live

    row = jnp.broadcast_to(jnp.arange(local_k, dtype=jnp.int32)[:, None], (local_k, slots))
    flat = lambda u, v: jnp.concatenate([u.reshape(-1), v.reshape(-1)])
    length = 2 * local_k * slots + q_count
    length = (length + UNROLL - 1) // UNROLL * UNROLL

    def listing(u, v, u_slot, v_slot, u_valid, v_valid):
        return pair_list(
            flat(u_slot, v_slot),
            flat(row, row + local_k),
            flat(u[2], v[2]),
            flat(u[3] & u_valid, v[3] & v_valid),
            q_count,
            length,
            2 * local_k,
        )

    own_t, sib_t = columns(table), columns(table_s)
    own_cross, sib_cross = own_t[0] == 2 - 2 * core, sib_t[0] == 2 * core
    near_list, near_rounds = listing(
        own_t,
        sib_t,
        own_t[1] + local_k * own_cross,
        sib_t[1] + local_k * (sib_t[0] == 1),
        own_cross | (own_t[0] == 1),
        sib_cross | (sib_t[0] == 1),
    )

    sums = jax.ShapeDtypeStruct((2 * local_k, pair_count, trial_count), F32)
    work = [
        VMEM((2 * local_k, trial_count, width), BF16),
        VMEM((2 * local_k + 1, trial_count, width), F32),
    ]

    def params():
        return pltpu.CompilerParams(vmem_limit_bytes=12 << 20)

    def cost(count, pairs):
        return pl.CostEstimate(
            flops=4 * count * pairs * width * width * trial_count, transcendentals=0, bytes_accessed=1 << 20
        )

    a_t, p_t = columns(pick(table, table_s)), columns(table_p)
    far_list, far_rounds = listing(a_t, p_t, a_t[1] + local_k, p_t[1], a_t[0] == 0, p_t[0] == 2)
    near_rounds, far_list, far_rounds = lax.optimization_barrier((near_rounds, far_list, far_rounds))
    near_rounds = density.before(near_rounds)
    if groups > 1:
        near_rounds = send_group(1, near_rounds)
    near, w_half = pl.pallas_call(
        functools.partial(near_kernel, 0, 1, True),
        out_shape=(sums, jax.ShapeDtypeStruct((q_count, half_g, width), BF16)),
        in_specs=[IN_SMEM] * 3 + [IN_VMEM] * 4 + [ANYWHERE],
        out_specs=(IN_VMEM, IN_VMEM),
        scratch_shapes=work + [pltpu.SemaphoreType.DMA((groups,))],
        compiler_params=params(),
        cost_estimate=cost(1, 160),
    )(core_id, near_list, near_rounds, pair_density, trial_vectors, sib, vec_s, screen)
    edge_vec, near = lax.optimization_barrier((pick(vec_s, trial_vectors), near))
    vec_p = lax.ppermute(edge_vec, "ka", onward)
    near, *came[0] = lax.optimization_barrier((near, *came[0]))
    for start, count, going in ((1, 1, range(2, min(groups, 3))), (2, groups - 2, range(3, groups))):
        if count < 1 or start >= groups:
            continue
        for g in going:
            near = send_group(g, near)
        near = pl.pallas_call(
            functools.partial(near_kernel, start, count, False),
            out_shape=sums,
            in_specs=[IN_SMEM] * 3 + [IN_VMEM] * 6,
            out_specs=IN_VMEM,
            scratch_shapes=work,
            input_output_aliases={8: 0},
            compiler_params=params(),
            cost_estimate=cost(count, 160),
        )(core_id, near_list, near_rounds, pair_density, trial_vectors, sib, vec_s, w_half, near)
        near = density.after(near)
    near, far_rounds = lax.optimization_barrier((near, far_rounds))
    far = None
    for c in range(groups):
        far = pl.pallas_call(
            functools.partial(far_kernel, c, 1, c == 0, len(came[c])),
            out_shape=sums,
            in_specs=[IN_SMEM] * 3 + [IN_VMEM] * (6 + (c > 0)) + [ANYWHERE] * len(came[c]),
            out_specs=IN_VMEM,
            scratch_shapes=work
            + [VMEM((local_k, pair_count, width), BF16), pltpu.SemaphoreType.DMA],
            input_output_aliases={9: 0} if c else {},
            compiler_params=params(),
            cost_estimate=cost(1, 80),
        )(
            core_id, far_list, far_rounds, pair_density, trial_vectors, sib, vec_s, w_half, vec_p,
            *([far] if c else []), *came[c],
        )
        if c in (groups - 3, groups - 1):
            far = density.after(far)
    screened2 = (2.0 * my_coulomb[None, :] * density.finish().astype(F32)).astype(BF16)
    half_sums = jax.ShapeDtypeStruct((local_k, pair_count, trial_count), F32)
    give, edge, inner = pl.pallas_call(
        last_kernel,
        out_shape=(jax.ShapeDtypeStruct(sums.shape, BF16), half_sums, half_sums),
        in_specs=[IN_SMEM] + [IN_VMEM] * 5,
        out_specs=(IN_VMEM,) * 3,
        compiler_params=params(),
        cost_estimate=cost(1, 16),
    )(core_id, pair_density, sib, screened2, near, far)

    got = lax.ppermute(give, "ka", sibling)
    edge, inner = edge + got[:local_k].astype(F32), inner + got[local_k:].astype(F32)
    rows = pair_count // parts
    rows_of = lambda value, at: lax.dynamic_slice_in_dim(value, at * rows, rows, 1)
    stay = lambda first: [(i, i) for i in range(first, size, 2)]
    back = [(i, (i - 2) % size) for i in range(1, size, 2)]

    def sent(value, steps, ka_pairs):
        pairs = [
            (s * parts + g, d * parts + (g + steps) % parts) for s, d in ka_pairs for g in range(parts)
        ]
        return lax.ppermute(
            rows_of(value, (mine + steps) % parts).astype(BF16), ("ka", "ga"), pairs
        ).astype(F32)

    answer = jnp.where(core == 0, rows_of(edge, mine), rows_of(inner, mine))
    answer = answer + sent(edge, 0, back)
    for steps in range(1, parts):
        answer = answer + sent(edge, steps, stay(0) + back) + sent(inner, steps, stay(1))
    energy_rows = lax.dynamic_slice_in_dim(energy, mine * rows, rows, 1)
    vector_rows = lax.dynamic_slice_in_dim(trial_vectors, mine * rows, rows, 1)
    return (energy_rows[:, :, None] * vector_rows.astype(F32) + answer).astype(BF16)


def solution(mesh):
    in_specs = (
        P("ka", None, "ga"),
        P("ka", None, None),
        P("ka", None),
        P("ga"),
        P(None, "ga", None),
        P("ka", None),
        P("ka"),
        P("ka", None),
    )
    out_specs = P("ka", "ga", None)
    return jax.shard_map(
        on_device, mesh=mesh, in_specs=in_specs, out_specs=out_specs, check_vma=False
    )
```

```python
import functools

import jax
import jax.numpy as jnp
from jax import lax
from jax.experimental import pallas as pl
from jax.experimental.pallas import tpu as pltpu
from jax.sharding import PartitionSpec as P

UNROLL = 32
F32, BF16 = jnp.float32, jnp.bfloat16
VMEM, SMEM = pltpu.VMEM, pltpu.SMEM
IN_VMEM, IN_SMEM, ANYWHERE = (pl.BlockSpec(memory_space=space) for space in (VMEM, SMEM, pl.ANY))


def pair_list(n_slot, k_slot, q, valid, q_count, length, spare):
    entries = q.shape[0]
    order = jnp.arange(entries, dtype=jnp.int32)
    qs = jnp.arange(q_count, dtype=jnp.int32)
    same = (q[:, None] == q[None, :]) & valid[None, :] & (order[None, :] < order[:, None])
    within = jnp.sum(same.astype(jnp.int32), axis=1)
    count = jnp.sum(((q[None, :] == qs[:, None]) & valid[None, :]).astype(jnp.int32), axis=1)
    padded = (count + 1) // 2 * 2
    base = jnp.sum(jnp.where(qs[None, :] < q[:, None], padded[None, :], 0), axis=1)
    place = jnp.where(valid, base + within, -1)
    code = n_slot + 64 * k_slot + 4096 * q
    blank = 64 * spare
    rows = jnp.arange(length, dtype=jnp.int32)
    listed = blank + jnp.sum(jnp.where(place[None, :] == rows[:, None], code[None, :] - blank, 0), axis=1)
    pairs = jnp.sum(padded)
    left = pairs % UNROLL
    rounds = (pairs + UNROLL // 2 - 1) // UNROLL * 2 + ((left > 0) & (left <= UNROLL // 2)).astype(jnp.int32)
    return listed, rounds[None]


def dot_last(u, v):
    return lax.dot_general(u, v, (((1,), (1,)), ((), ())), preferred_element_type=F32)


def one_group(listed, rounds, w_ref, row, slabs, vectors, out_ref, prod, total, first):
    trials = prod.shape[1]
    width = prod.shape[2]
    slots = prod.shape[0]

    for n in range(slots):
        made = lax.dot_general(vectors(n), slabs(n), (((0,), (0,)), ((), ())), preferred_element_type=F32)
        prod[n] = made.astype(BF16)
    total[...] = jnp.zeros_like(total)

    def some(start, count):
        for d in range(0, count, 2):
            a, b = listed[start + d], listed[start + d + 1]
            both = jnp.concatenate([prod[a & 63], prod[b & 63]], axis=0)
            made = dot_last(both, w_ref[a >> 12, pl.ds(row, width), :])
            total[(a >> 6) & 63] += made[:trials]
            total[(b >> 6) & 63] += made[trials:]

    def whole_round(i, _):
        some(i * UNROLL, UNROLL)
        return 0

    lax.fori_loop(0, rounds[0] >> 1, whole_round, 0)

    @pl.when((rounds[0] & 1) == 1)
    def _():
        some((rounds[0] >> 1) * UNROLL, UNROLL // 2)

    for k in range(slots):
        made = dot_last(slabs(k), total[k].astype(BF16))

        if first:
            out_ref[k] = made
        else:
            out_ref[k] += made


def pack_kernel(core, source, give, first, second, sems):
    half_g, width = give.shape[2], first.shape[2]
    part = source.shape[0] // 4
    away = pl.multiple_of((1 - core[0]) * half_g, half_g)
    copies = [
        pltpu.make_async_copy(
            source.at[pl.ds(j * part, part), :, pl.ds(start, out.shape[2])], out.at[pl.ds(j * part, part)], sems.at[i, j]
        )
        for i, (start, out) in enumerate(((away, give), (0, first), (half_g, second)))
        for j in range(4)
    ]
    for copy in copies:
        copy.start()
    for copy in copies:
        copy.wait()


def density_kernel(core, own, vec, sib, vec_s, out):
    half_g = sib.shape[2]
    rows = lambda value: value.reshape(value.shape[0] * value.shape[1], value.shape[2])

    def over_pairs(v, d):
        return lax.dot_general(rows(v), rows(d), (((0,), (0,)), ((), ())), preferred_element_type=F32)

    mine = own[:, :, pl.ds(pl.multiple_of(core[0] * half_g, half_g), half_g)]
    out[...] = over_pairs(vec[...], mine) + over_pairs(vec_s[...], sib[...])


def near_kernel(start, count, load, *refs):
    if load:
        core, listed, rounds, own, vec, sib, vec_s, screen, out, w, prod, total, sems = refs
    else:
        core, listed, rounds, own, vec, sib, vec_s, w, _, out, prod, total = refs
    half, _, _ = own.shape
    width = prod.shape[2]
    half_g = w.shape[1]
    groups = half_g // width
    own_at = core[0] * half_g

    def copy(g):
        return pltpu.make_async_copy(
            screen.at[:, pl.ds(pl.multiple_of(own_at + g * width, width), width), :],
            w.at[:, pl.ds(g * width, width), :],
            sems.at[g],
        )

    if load:
        for g in range(groups):
            copy(g).start()
    for g in range(start, start + count):
        if load:
            copy(g).wait()
        at = pl.multiple_of(own_at + g * width, width)

        def slabs(n, at=at, g=g):
            return own[n, :, pl.ds(at, width)] if n < half else sib[n - half, :, g * width : (g + 1) * width]

        def vectors(n):
            return vec[n] if n < half else vec_s[n - half]

        one_group(listed, rounds, w, g * width, slabs, vectors, out, prod, total, load and g == start)
    if load:
        for g in range(start + count, groups):
            copy(g).wait()


def far_kernel(start, count, fresh, sources, core, listed, rounds, own, vec, sib, vec_s, w, vec_p, *refs):
    refs = refs[0 if fresh else 1 :]
    sources, (out, prod, total, came, sem) = refs[:sources], refs[sources:]
    half, _, _ = own.shape
    width = prod.shape[2]
    half_g = w.shape[1]
    own_at = core[0] * half_g
    if len(sources) == 1:
        pltpu.make_async_copy(sources[0], came, sem).start()
    else:

        @pl.when(core[0] == 0)
        def _():
            pltpu.make_async_copy(sources[0], came, sem).start()

        @pl.when(core[0] != 0)
        def _():
            pltpu.make_async_copy(sources[1], came, sem).start()

    pltpu.make_async_copy(sources[0], came, sem).wait()
    for g in range(start, start + count):
        at = pl.multiple_of(own_at + g * width, width)

        def slabs(n, at=at, g=g):
            if n >= half:
                return came[n - half, :, (g - start) * width : (g - start + 1) * width]
            return jnp.where(
                core[0] == 0, own[n, :, pl.ds(at, width)], sib[n, :, g * width : (g + 1) * width]
            )

        def vectors(n):
            if n >= half:
                return vec_p[n - half]
            return jnp.where(core[0] == 0, vec[n], vec_s[n])

        one_group(listed, rounds, w, g * width, slabs, vectors, out, prod, total, fresh and g == start)


def last_kernel(core, own, sib, s2, near, far, give, edge, inner):
    half, pairs, _ = own.shape
    trials, half_g = s2.shape
    width = 256
    own_at = core[0] * half_g

    def exchange(slab):
        acc = jnp.zeros((half * pairs, trials), F32)
        for g in range(half_g // width):
            acc += dot_last(slab(g).reshape(half * pairs, width), s2[:, g * width : (g + 1) * width])
        return acc.reshape(half, pairs, trials)

    mine = exchange(lambda g: own[:, :, pl.ds(pl.multiple_of(own_at + g * width, width), width)]) - near[:half]
    other = exchange(lambda g: sib[:, :, g * width : (g + 1) * width]) - near[half:]

    @pl.when(core[0] == 0)
    def _():
        edge[...] = mine - far[:half]
        inner[...] = other
        give[:half] = (-far[half:]).astype(BF16)
        give[half:] = other.astype(BF16)

    @pl.when(core[0] != 0)
    def _():
        edge[...] = -far[half:]
        inner[...] = mine
        give[:half] = (other - far[:half]).astype(BF16)
        give[half:] = mine.astype(BF16)


def density_steps(part, me, size):
    low = [i for i in range(size) if (i // 2) % 2 == 0]
    part = part + (yield part.astype(BF16), [(i ^ 2, i) for i in low]).astype(F32)
    bit = 4
    while bit < size:
        part = part + (yield part.astype(BF16), [(i, i ^ bit) for i in low]).astype(F32)
        bit *= 2
    part = part.astype(BF16)
    other = yield part, [(i, i ^ 2) for i in low]
    return jnp.where((me // 2) % 2 == 0, part, other)


class Density:
    def __init__(self, steps):
        self.steps, self.result = steps, None
        self.send(None)

    def send(self, got):
        try:
            self.give, self.pairs = self.steps.send(got)
        except StopIteration as stop:
            self.give, self.result = stop.value, stop.value

    def after(self, value):
        if self.result is None:
            came = lax.ppermute(self.give, "ka", self.pairs)
            came, value = lax.optimization_barrier((came, value))
            self.send(came)
        return self.before(value)

    def before(self, value):
        self.give, value = lax.optimization_barrier((self.give, value))
        return value

    def finish(self):
        while self.result is None:
            self.after(jnp.zeros((1,), F32))
        return self.give


def on_device(pair_density, trial_vectors, energy, coulomb, screen, neighbors, live_count, q_index):
    local_k, pair_count, local_g = pair_density.shape
    trial_count = trial_vectors.shape[2]
    q_count, _, width = screen.shape
    slots = neighbors.shape[1]
    size, parts = lax.axis_size("ka"), lax.axis_size("ga")
    me, mine = lax.axis_index("ka"), lax.axis_index("ga")
    core = me % 2
    core_id = core.astype(jnp.int32)[None]
    half_g = local_g // 2
    groups = half_g // width
    sibling = [(i, i ^ 1) for i in range(size)]
    onward = [(i, (i + 2) % size) for i in range(size)]
    to_next = [[(i, (i + 1 + target) % size) for i in range(1, size, 2)] for target in range(2)]

    def pick(first, second):
        return jnp.where(core == 0, first, second)

    offset = (neighbors // local_k - me + 1) % size
    table = jnp.concatenate([offset * local_k + neighbors % local_k, q_index, live_count[:, None]], axis=1)
    table_s = lax.ppermute(table, "ka", sibling)
    vec_s = lax.ppermute(trial_vectors, "ka", sibling)
    edge = pick(table_s, table)
    table_p = lax.ppermute(edge, "ka", onward)

    sent = lambda last: jax.ShapeDtypeStruct((local_k, pair_count, last), BF16)
    give_half, *first_pieces = pl.pallas_call(
        pack_kernel,
        out_shape=(sent(half_g), sent(width), sent(width)),
        in_specs=[IN_SMEM, ANYWHERE],
        out_specs=(IN_VMEM,) * 3,
        scratch_shapes=[pltpu.SemaphoreType.DMA((3, 4))],
    )(core_id, pair_density)
    *first_pieces, _ = lax.optimization_barrier((*first_pieces, edge))
    sib = lax.ppermute(give_half, "ka", sibling)
    own_half = lax.dynamic_slice_in_dim(pair_density, core * half_g, half_g, 2)
    came = [[lax.ppermute(piece, "ka", pairs) for piece, pairs in zip(first_pieces, to_next)]]

    def send_group(g, value):
        piece = pick(sib[:, :, g * width : (g + 1) * width], own_half[:, :, g * width : (g + 1) * width])
        piece, value = lax.optimization_barrier((piece, value))
        came.append([lax.ppermute(piece, "ka", onward)])
        piece, value = lax.optimization_barrier((piece, value))
        return value

    part = pl.pallas_call(
        density_kernel,
        out_shape=jax.ShapeDtypeStruct((trial_count, half_g), F32),
        in_specs=[IN_SMEM] + [IN_VMEM] * 4,
        out_specs=IN_VMEM,
        compiler_params=pltpu.CompilerParams(vmem_limit_bytes=12 << 20),
    )(core_id, pair_density, trial_vectors, sib, vec_s)
    density = Density(density_steps(part, me, size))
    my_coulomb = lax.dynamic_slice_in_dim(coulomb, core * half_g, half_g, 0)

    def columns(t):
        live = jnp.arange(slots, dtype=jnp.int32)[None, :] < t[:, 2 * slots :]
        near = t[:, :slots]
        return near // local_k, near % local_k, t[:, slots : 2 * slots], live

    row = jnp.broadcast_to(jnp.arange(local_k, dtype=jnp.int32)[:, None], (local_k, slots))
    flat = lambda u, v: jnp.concatenate([u.reshape(-1), v.reshape(-1)])
    length = 2 * local_k * slots + q_count
    length = (length + UNROLL - 1) // UNROLL * UNROLL

    def listing(u, v, u_slot, v_slot, u_valid, v_valid):
        return pair_list(
            flat(u_slot, v_slot),
            flat(row, row + local_k),
            flat(u[2], v[2]),
            flat(u[3] & u_valid, v[3] & v_valid),
            q_count,
            length,
            2 * local_k,
        )

    own_t, sib_t = columns(table), columns(table_s)
    own_cross, sib_cross = own_t[0] == 2 - 2 * core, sib_t[0] == 2 * core
    near_list, near_rounds = listing(
        own_t,
        sib_t,
        own_t[1] + local_k * own_cross,
        sib_t[1] + local_k * (sib_t[0] == 1),
        own_cross | (own_t[0] == 1),
        sib_cross | (sib_t[0] == 1),
    )

    sums = jax.ShapeDtypeStruct((2 * local_k, pair_count, trial_count), F32)
    work = [
        VMEM((2 * local_k, trial_count, width), BF16),
        VMEM((2 * local_k + 1, trial_count, width), F32),
    ]

    def params():
        return pltpu.CompilerParams(vmem_limit_bytes=12 << 20)

    def cost(count, pairs):
        return pl.CostEstimate(
            flops=4 * count * pairs * width * width * trial_count, transcendentals=0, bytes_accessed=1 << 20
        )

    a_t, p_t = columns(pick(table, table_s)), columns(table_p)
    far_list, far_rounds = listing(a_t, p_t, a_t[1] + local_k, p_t[1], a_t[0] == 0, p_t[0] == 2)
    near_rounds, far_list, far_rounds = lax.optimization_barrier((near_rounds, far_list, far_rounds))
    near_rounds = density.before(near_rounds)
    if groups > 1:
        near_rounds = send_group(1, near_rounds)
    near, w_half = pl.pallas_call(
        functools.partial(near_kernel, 0, 1, True),
        out_shape=(sums, jax.ShapeDtypeStruct((q_count, half_g, width), BF16)),
        in_specs=[IN_SMEM] * 3 + [IN_VMEM] * 4 + [ANYWHERE],
        out_specs=(IN_VMEM, IN_VMEM),
        scratch_shapes=work + [pltpu.SemaphoreType.DMA((groups,))],
        compiler_params=params(),
        cost_estimate=cost(1, 160),
    )(core_id, near_list, near_rounds, pair_density, trial_vectors, sib, vec_s, screen)
    edge_vec, near = lax.optimization_barrier((pick(vec_s, trial_vectors), near))
    vec_p = lax.ppermute(edge_vec, "ka", onward)
    near, *came[0] = lax.optimization_barrier((near, *came[0]))
    for start, count, going in ((1, 1, range(2, min(groups, 3))), (2, groups - 2, range(3, groups))):
        if count < 1 or start >= groups:
            continue
        for g in going:
            near = send_group(g, near)
        near = pl.pallas_call(
            functools.partial(near_kernel, start, count, False),
            out_shape=sums,
            in_specs=[IN_SMEM] * 3 + [IN_VMEM] * 6,
            out_specs=IN_VMEM,
            scratch_shapes=work,
            input_output_aliases={8: 0},
            compiler_params=params(),
            cost_estimate=cost(count, 160),
        )(core_id, near_list, near_rounds, pair_density, trial_vectors, sib, vec_s, w_half, near)
        near = density.after(near)
    near, far_rounds = lax.optimization_barrier((near, far_rounds))
    far = None
    for c in range(groups):
        far = pl.pallas_call(
            functools.partial(far_kernel, c, 1, c == 0, len(came[c])),
            out_shape=sums,
            in_specs=[IN_SMEM] * 3 + [IN_VMEM] * (6 + (c > 0)) + [ANYWHERE] * len(came[c]),
            out_specs=IN_VMEM,
            scratch_shapes=work
            + [VMEM((local_k, pair_count, width), BF16), pltpu.SemaphoreType.DMA],
            input_output_aliases={9: 0} if c else {},
            compiler_params=params(),
            cost_estimate=cost(1, 80),
        )(
            core_id, far_list, far_rounds, pair_density, trial_vectors, sib, vec_s, w_half, vec_p,
            *([far] if c else []), *came[c],
        )
        if c in (groups - 3, groups - 1):
            far = density.after(far)
    screened2 = (2.0 * my_coulomb[None, :] * density.finish().astype(F32)).astype(BF16)
    half_sums = jax.ShapeDtypeStruct((local_k, pair_count, trial_count), F32)
    give, edge, inner = pl.pallas_call(
        last_kernel,
        out_shape=(jax.ShapeDtypeStruct(sums.shape, BF16), half_sums, half_sums),
        in_specs=[IN_SMEM] + [IN_VMEM] * 5,
        out_specs=(IN_VMEM,) * 3,
        compiler_params=params(),
        cost_estimate=cost(1, 16),
    )(core_id, pair_density, sib, screened2, near, far)

    got = lax.ppermute(give, "ka", sibling)
    edge, inner = edge + got[:local_k].astype(F32), inner + got[local_k:].astype(F32)
    rows = pair_count // parts
    rows_of = lambda value, at: lax.dynamic_slice_in_dim(value, at * rows, rows, 1)
    stay = lambda first: [(i, i) for i in range(first, size, 2)]
    back = [(i, (i - 2) % size) for i in range(1, size, 2)]

    def sent(value, steps, ka_pairs):
        pairs = [
            (s * parts + g, d * parts + (g + steps) % parts) for s, d in ka_pairs for g in range(parts)
        ]
        return lax.ppermute(
            rows_of(value, (mine + steps) % parts).astype(BF16), ("ka", "ga"), pairs
        ).astype(F32)

    answer = jnp.where(core == 0, rows_of(edge, mine), rows_of(inner, mine))
    answer = answer + sent(edge, 0, back)
    for steps in range(1, parts):
        answer = answer + sent(edge, steps, stay(0) + back) + sent(inner, steps, stay(1))
    energy_rows = lax.dynamic_slice_in_dim(energy, mine * rows, rows, 1)
    vector_rows = lax.dynamic_slice_in_dim(trial_vectors, mine * rows, rows, 1)
    return (energy_rows[:, :, None] * vector_rows.astype(F32) + answer).astype(BF16)


def solution(mesh):
    in_specs = (
        P("ka", None, "ga"),
        P("ka", None, None),
        P("ka", None),
        P("ga"),
        P(None, "ga", None),
        P("ka", None),
        P("ka"),
        P("ka", None),
    )
    out_specs = P("ka", "ga", None)
    return jax.shard_map(
        on_device, mesh=mesh, in_specs=in_specs, out_specs=out_specs, check_vma=False
    )
```
